32 devices in a mesh: section: 2 (over core), ctx: 4 (over y, x), wt: 4 (over z).
Axes of the slice: x: 2, y: 2, z: 4, core: 2. Of those that a mesh axis runs over, the one named last changes fastest.
Arguments:
- inputs: bfloat16 [2, 1024, 576], P(None, ('ctx', 'wt')), may hold values from -6 to 6
- doc_start: int32 [2, 1024], replicated, may hold values from 0 to 1791, as said below
- attn_gain: float32 [2, 576], P('section'), may hold values from 0.25 to 1.75
- w_q: bfloat16 [2, 576, 576], P('section', 'wt'), may hold values from -0.25 to 0.25
- key_projection: bfloat16 [2, 576, 192], P('section', 'wt'), may hold values from -0.25 to 0.25
- value_projection: bfloat16 [2, 576, 192], P('section', 'wt'), may hold values from -0.25 to 0.25
- w_o: bfloat16 [2, 576, 576], P('section', 'wt'), may hold values from -1.5 to 1.5
- mlp_gain: float32 [2, 576], P('section'), may hold values from 0.25 to 1.75
- w_gate: bfloat16 [2, 576, 1536], P('section', None, 'wt'), may hold values from -0.25 to 0.25
- w_up: bfloat16 [2, 576, 1536], P('section', None, 'wt'), may hold values from -0.25 to 0.25
- w_down: bfloat16 [2, 1536, 576], P('section', 'wt'), may hold values from -0.15625 to 0.15625
- cotangent: float32 [2, 1024, 576], P(None, ('ctx', 'wt')), may hold values from -6 to 6
Outputs:
- acts: bfloat16 [2, 2, 1024, 576], P('section', None, ('ctx', 'wt'))
- dacts: bfloat16 [2, 2, 1024, 576], P('section', None, ('ctx', 'wt'))
- grad_attn_gain: float32 [2, 576], P('section', 'wt')
- grad_w_q: float32 [2, 576, 576], P('section', 'wt')
- grad_w_k: float32 [2, 576, 192], P('section', 'wt')
- grad_w_v: float32 [2, 576, 192], P('section', 'wt')
- grad_w_o: float32 [2, 576, 576], P('section', 'wt')
- grad_mlp_gain: float32 [2, 576], P('section', 'wt')
- grad_w_gate: float32 [2, 576, 1536], P('section', None, 'wt')
- grad_w_up: float32 [2, 576, 1536], P('section', None, 'wt')
- grad_w_down: float32 [2, 1536, 576], P('section', 'wt')
The draws below stay inside these ranges and needn't reach their ends.
Inputs may be any that keep to these rules, and one draw needn't show every extreme that they name: `doc_start`: doc_start_i is the first position of token i's document in the sequence of 2048 tokens: never above i, never falling along the sequence, equal within a document; three documents, the last beginning at position 1791.
All inputs are finite; a program needn't handle non-finite values.
Results may differ from the reference program's by a relative error of at most 0.028.
Values may be sent and summed in bfloat16 or wider, within the bound.
A program may use at most 128 MiB of HBM per device.

```python
import math
import jax
import jax.numpy as jnp
from jax import lax

MODEL_DIMENSION = 576
QUERY_HEAD_COUNT = 9
KEY_VALUE_HEADS = 3
HEAD_DIMENSION = 64
FF = 1536
M = 2
TOK_MB = 1024


def draw_doc_start(key, part):
    running_sum = M * TOK_MB
    second_bound = running_sum - running_sum // 8 - 1
    first_bound = jax.random.randint(key, (), running_sum // 8, second_bound)
    positions = jnp.arange(running_sum, dtype=jnp.int32)
    starts = jnp.where(positions >= second_bound, second_bound, jnp.where(positions >= first_bound, first_bound, 0))
    return starts.reshape(M, TOK_MB).astype(jnp.int32)


def steps_of(key, shape, pieces, low, top_value):
    def one(position, blocks):
        draws = jax.random.uniform(jax.random.fold_in(jax.random.fold_in(key, 6), position), (blocks,), jnp.float32, low / len(pieces), top_value / len(pieces))
        return jnp.repeat(jnp.exp(draws), shape[position] // blocks).reshape((-1,) + (1,) * (len(shape) - position - 1))

    gain = one(*pieces[0])
    for cut in pieces[1:]:
        gain = gain * one(*cut)
    return gain


def normal_values(rng, extent, deviation, most, shards=(), kind=jnp.bfloat16):
    gain = steps_of(rng, extent, shards, -0.22, 0.18) if shards else 1.0
    drawn = jax.random.normal(rng, extent, jnp.float32) * deviation * gain
    return jnp.minimum(jnp.maximum(drawn, -most), most).astype(kind)


def setup_inputs(seed: int = 0) -> dict:
    key_of = jax.random.split(jax.random.key(seed), 13)
    inputs = normal_values(key_of[0], (M, TOK_MB, MODEL_DIMENSION), 1.0, 6.0, ((1, 16),))
    doc_start = draw_doc_start(jax.random.fold_in(key_of[12], 71), 0)
    attn_gain = jnp.clip(1.0 + 0.15 * jax.random.normal(key_of[2], (2, MODEL_DIMENSION), jnp.float32), 0.25, 1.75)
    w_q = normal_values(key_of[3], (2, MODEL_DIMENSION, MODEL_DIMENSION), MODEL_DIMENSION ** -0.5, 0.25, ((0, 2), (1, 4)))
    key_projection = normal_values(key_of[4], (2, MODEL_DIMENSION, KEY_VALUE_HEADS * HEAD_DIMENSION), MODEL_DIMENSION ** -0.5, 0.25, ((0, 2), (1, 4)))
    value_projection = normal_values(key_of[5], (2, MODEL_DIMENSION, KEY_VALUE_HEADS * HEAD_DIMENSION), MODEL_DIMENSION ** -0.5, 0.25, ((0, 2), (1, 4)))
    w_o = normal_values(key_of[6], (2, MODEL_DIMENSION, MODEL_DIMENSION), (MODEL_DIMENSION // 32) ** -0.5, 1.5, ((0, 2), (1, 4)))
    mlp_gain = jnp.clip(1.0 + 0.15 * jax.random.normal(key_of[7], (2, MODEL_DIMENSION), jnp.float32), 0.25, 1.75)
    w_gate = normal_values(key_of[8], (2, MODEL_DIMENSION, FF), MODEL_DIMENSION ** -0.5, 0.25, ((0, 2), (2, 4)))
    w_up = normal_values(key_of[9], (2, MODEL_DIMENSION, FF), MODEL_DIMENSION ** -0.5, 0.25, ((0, 2), (2, 4)))
    w_down = normal_values(key_of[10], (2, FF, MODEL_DIMENSION), FF ** -0.5, 0.15625, ((0, 2), (1, 4)))
    cotangent = normal_values(key_of[11], (M, TOK_MB, MODEL_DIMENSION), 1.0, 6.0, ((1, 16),), jnp.float32)
    return {"inputs": inputs, "doc_start": doc_start, "attn_gain": attn_gain, "w_q": w_q, "key_projection": key_projection, "value_projection": value_projection, "w_o": w_o, "mlp_gain": mlp_gain, "w_gate": w_gate, "w_up": w_up, "w_down": w_down, "cotangent": cotangent}


EPSILON = 1e-05
THETA = 100000.0
MASKED_FLOOR = -1e+30

def rounded(value_matrix):
    return lax.optimization_barrier(value_matrix.astype(jnp.bfloat16)).astype(jnp.float32)

def rope_tables(rotary):
    half_size = HEAD_DIMENSION // 2
    inverse = 1.0 / THETA ** (jnp.arange(half_size).astype(jnp.float32) * 2.0 / HEAD_DIMENSION)
    angles = rotary[:, None] * inverse[None, :]
    return (jnp.concatenate([jnp.cos(angles), jnp.cos(angles)], -1), jnp.concatenate([jnp.sin(angles), jnp.sin(angles)], -1))

def apply_rotation(value_matrix, cosine_values, sine_values):
    half_size = value_matrix.shape[-1] // 2
    turned = jnp.concatenate([-value_matrix[..., half_size:], value_matrix[..., :half_size]], -1)
    return value_matrix * cosine_values[:, None, :] + turned * sine_values[:, None, :]

def reverse_rotation(grads, cosine_values, sine_values):
    half_size = grads.shape[-1] // 2
    scaled = grads * sine_values[:, None, :]
    turned = jnp.concatenate([scaled[..., half_size:], -scaled[..., :half_size]], -1)
    return grads * cosine_values[:, None, :] + turned

def row_product(left_matrix, right_matrix):
    return lax.dot_general(left_matrix, right_matrix, (((0,), (0,)), ((), ())), preferred_element_type=jnp.float32)

def back_product(left_matrix, right_matrix):
    return lax.dot_general(left_matrix, right_matrix, (((1,), (1,)), ((), ())), preferred_element_type=jnp.float32)

def block_scores(rows_of_queries, key_rows, lower_limit, doc_flat):
    tally_count = rows_of_queries.shape[0]
    span = key_rows.shape[0]
    heads_of_queries = rows_of_queries.astype(jnp.float32).reshape(tally_count, KEY_VALUE_HEADS, QUERY_HEAD_COUNT // KEY_VALUE_HEADS, HEAD_DIMENSION)
    scores = jnp.einsum('qhge,khe->hgqk', heads_of_queries, key_rows.astype(jnp.float32)) * 0.125
    query_pos = lower_limit + jnp.arange(tally_count, dtype=jnp.int32)
    key_pos = jnp.arange(span, dtype=jnp.int32)
    query_doc = doc_flat[lower_limit:lower_limit + tally_count]
    allowed = (key_pos[None, :] <= query_pos[:, None]) & (key_pos[None, :] >= query_doc[:, None])
    return jnp.where(allowed[None, None], scores, MASKED_FLOOR)

def layer_forward(section_in, doc_flat, cosine_values, sine_values, params):
    attn_gain, w_q, key_projection, value_projection, w_o, mlp_gain, w_gate, w_up, w_down = params
    running_sum = section_in.shape[0]
    hidden = section_in.astype(jnp.float32)
    inverse1 = lax.rsqrt(lax.optimization_barrier(jnp.mean(hidden * hidden, -1, keepdims=True)) + EPSILON)
    normed1 = hidden * inverse1
    attention_input = (normed1 * attn_gain).astype(jnp.bfloat16)
    query_matrix = apply_rotation(jnp.dot(attention_input, w_q, preferred_element_type=jnp.float32).reshape(running_sum, QUERY_HEAD_COUNT, HEAD_DIMENSION), cosine_values, sine_values).astype(jnp.bfloat16)
    key_matrix = apply_rotation(jnp.dot(attention_input, key_projection, preferred_element_type=jnp.float32).reshape(running_sum, KEY_VALUE_HEADS, HEAD_DIMENSION), cosine_values, sine_values).astype(jnp.bfloat16)
    value_matrix = jnp.dot(attention_input, value_projection, preferred_element_type=jnp.float32).astype(jnp.bfloat16).reshape(running_sum, KEY_VALUE_HEADS, HEAD_DIMENSION)
    rows_per_block = math.gcd(running_sum, 512)
    mixed_parts = []
    log_parts = []
    for block_index in range(running_sum // rows_per_block):
        lower_limit = block_index * rows_per_block
        upper_limit = lower_limit + rows_per_block
        scores = block_scores(query_matrix[lower_limit:upper_limit], key_matrix[:upper_limit], lower_limit, doc_flat)
        row_top = lax.optimization_barrier(jnp.max(scores, -1))
        weights = jnp.exp(scores - row_top[..., None])
        summed = lax.optimization_barrier(jnp.sum(weights, -1))
        accumulated = jnp.einsum('hgqk,khe->hgqe', rounded(weights), value_matrix[:upper_limit].astype(jnp.float32))
        mixed_parts.append((accumulated / summed[..., None]).transpose(2, 0, 1, 3).reshape(rows_per_block, QUERY_HEAD_COUNT * HEAD_DIMENSION))
        log_parts.append(row_top + jnp.log(summed))
    blended_output = jnp.concatenate(mixed_parts, 0).astype(jnp.bfloat16)
    log_total = jnp.concatenate(log_parts, -1)
    residual = hidden + jnp.dot(blended_output, w_o, preferred_element_type=jnp.float32)
    inverse2 = lax.rsqrt(lax.optimization_barrier(jnp.mean(residual * residual, -1, keepdims=True)) + EPSILON)
    normed2 = residual * inverse2
    mlp_in = (normed2 * mlp_gain).astype(jnp.bfloat16)
    gate_pre = jnp.dot(mlp_in, w_gate, preferred_element_type=jnp.float32)
    up_pre = jnp.dot(mlp_in, w_up, preferred_element_type=jnp.float32)
    activated = (gate_pre * jax.nn.sigmoid(gate_pre) * up_pre).astype(jnp.bfloat16)
    result = (residual + jnp.dot(activated, w_down, preferred_element_type=jnp.float32)).astype(jnp.bfloat16)
    saved_state = (normed1, inverse1, attention_input, query_matrix, key_matrix, value_matrix, blended_output, log_total, normed2, inverse2, mlp_in, gate_pre, up_pre, activated)
    return (result, saved_state)

def attention_backward(query_matrix, key_matrix, value_matrix, blended_output, log_total, attention_gradient, doc_flat):
    running_sum = query_matrix.shape[0]
    query_groups = QUERY_HEAD_COUNT // KEY_VALUE_HEADS
    delta_per_row = lax.optimization_barrier(jnp.sum((attention_gradient.astype(jnp.float32) * blended_output.astype(jnp.float32)).reshape(running_sum, KEY_VALUE_HEADS, query_groups, HEAD_DIMENSION), -1))
    key_gradient_sum = jnp.zeros((running_sum, KEY_VALUE_HEADS, HEAD_DIMENSION), jnp.float32)
    value_gradient_sum = jnp.zeros((running_sum, KEY_VALUE_HEADS, HEAD_DIMENSION), jnp.float32)
    query_parts = []
    rows_per_block = math.gcd(running_sum, 512)
    for block_index in range(running_sum // rows_per_block):
        lower_limit = block_index * rows_per_block
        upper_limit = lower_limit + rows_per_block
        scores = block_scores(query_matrix[lower_limit:upper_limit], key_matrix[:upper_limit], lower_limit, doc_flat)
        probabilities = jnp.exp(scores - log_total[:, :, lower_limit:upper_limit][..., None])
        head_gradients = attention_gradient[lower_limit:upper_limit].astype(jnp.float32).reshape(rows_per_block, KEY_VALUE_HEADS, query_groups, HEAD_DIMENSION)
        heads_of_queries = query_matrix[lower_limit:upper_limit].astype(jnp.float32).reshape(rows_per_block, KEY_VALUE_HEADS, query_groups, HEAD_DIMENSION)
        value_gradient_sum = value_gradient_sum.at[:upper_limit].add(jnp.einsum('hgqk,qhge->khe', rounded(probabilities), head_gradients))
        grad_probs = jnp.einsum('qhge,khe->hgqk', head_gradients, value_matrix[:upper_limit].astype(jnp.float32))
        block_delta = delta_per_row[lower_limit:upper_limit].transpose(1, 2, 0)
        grad_scores = rounded(probabilities * (grad_probs - block_delta[..., None]))
        query_parts.append(jnp.einsum('hgqk,khe->qhge', grad_scores, key_matrix[:upper_limit].astype(jnp.float32)) * 0.125)
        key_gradient_sum = key_gradient_sum.at[:upper_limit].add(jnp.einsum('hgqk,qhge->khe', grad_scores, heads_of_queries) * 0.125)
    grad_query = jnp.concatenate(query_parts, 0).reshape(running_sum, QUERY_HEAD_COUNT, HEAD_DIMENSION)
    return (grad_query, key_gradient_sum, value_gradient_sum)

def layer_backward(saved_state, upstream, doc_flat, cosine_values, sine_values, params):
    attn_gain, w_q, key_projection, value_projection, w_o, mlp_gain, w_gate, w_up, w_down = params
    normed1, inverse1, attention_input, query_matrix, key_matrix, value_matrix, blended_output, log_total, normed2, inverse2, mlp_in, gate_pre, up_pre, activated = saved_state
    running_sum = upstream.shape[0]
    out_grad = upstream.astype(jnp.bfloat16)
    grad_down = row_product(activated, out_grad)
    grad_activated = back_product(out_grad, w_down)
    sigmoid_gate = jax.nn.sigmoid(gate_pre)
    grad_gate_rows = (grad_activated * up_pre * sigmoid_gate * (1.0 + gate_pre * (1.0 - sigmoid_gate))).astype(jnp.bfloat16)
    grad_up_rows = (grad_activated * gate_pre * sigmoid_gate).astype(jnp.bfloat16)
    grad_gate = row_product(mlp_in, grad_gate_rows)
    grad_up = row_product(mlp_in, grad_up_rows)
    grad_mlp_in = back_product(grad_gate_rows, w_gate) + back_product(grad_up_rows, w_up)
    grad_mlp_gain = lax.optimization_barrier(jnp.sum(grad_mlp_in * normed2, 0))
    scaled2 = grad_mlp_in * mlp_gain
    grad_residual = upstream + inverse2 * (scaled2 - normed2 * lax.optimization_barrier(jnp.mean(scaled2 * normed2, -1, keepdims=True)))
    residual_grad = grad_residual.astype(jnp.bfloat16)
    grad_out = row_product(blended_output, residual_grad)
    attention_gradient = back_product(residual_grad, w_o).astype(jnp.bfloat16)
    grad_query, key_gradient_sum, value_gradient_sum = attention_backward(query_matrix, key_matrix, value_matrix, blended_output, log_total, attention_gradient, doc_flat)
    grad_queries = reverse_rotation(grad_query, cosine_values, sine_values).astype(jnp.bfloat16).reshape(running_sum, QUERY_HEAD_COUNT * HEAD_DIMENSION)
    key_gradients = reverse_rotation(key_gradient_sum, cosine_values, sine_values).astype(jnp.bfloat16).reshape(running_sum, KEY_VALUE_HEADS * HEAD_DIMENSION)
    value_gradients = value_gradient_sum.astype(jnp.bfloat16).reshape(running_sum, KEY_VALUE_HEADS * HEAD_DIMENSION)
    grad_query_w = row_product(attention_input, grad_queries)
    grad_key_w = row_product(attention_input, key_gradients)
    grad_value_w = row_product(attention_input, value_gradients)
    grad_attn_in = back_product(grad_queries, w_q) + back_product(key_gradients, key_projection) + back_product(value_gradients, value_projection)
    grad_attn_gain = lax.optimization_barrier(jnp.sum(grad_attn_in * normed1, 0))
    scaled1 = grad_attn_in * attn_gain
    grad_input = (grad_residual + inverse1 * (scaled1 - normed1 * lax.optimization_barrier(jnp.mean(scaled1 * normed1, -1, keepdims=True)))).astype(jnp.bfloat16)
    return (grad_input, (grad_attn_gain, grad_query_w, grad_key_w, grad_value_w, grad_out, grad_mlp_gain, grad_gate, grad_up, grad_down))

def reference(inputs, doc_start, attn_gain, w_q, key_projection, value_projection, w_o, mlp_gain, w_gate, w_up, w_down, cotangent):
    running_sum = M * TOK_MB
    doc_flat = doc_start.reshape(running_sum).astype(jnp.int32)
    rotary = (jnp.arange(running_sum, dtype=jnp.int32) - doc_flat).astype(jnp.float32)
    cosine_values, sine_values = rope_tables(rotary)
    first_params = tuple((item[0] for item in (attn_gain, w_q, key_projection, value_projection, w_o, mlp_gain, w_gate, w_up, w_down)))
    second_params = tuple((item[1] for item in (attn_gain, w_q, key_projection, value_projection, w_o, mlp_gain, w_gate, w_up, w_down)))
    first_out, first_saved = layer_forward(inputs.reshape(running_sum, MODEL_DIMENSION), doc_flat, cosine_values, sine_values, first_params)
    second_out, second_saved = layer_forward(first_out, doc_flat, cosine_values, sine_values, second_params)
    second_grad, second_grads = layer_backward(second_saved, cotangent.reshape(running_sum, MODEL_DIMENSION), doc_flat, cosine_values, sine_values, second_params)
    first_grad, first_grads = layer_backward(first_saved, second_grad.astype(jnp.float32), doc_flat, cosine_values, sine_values, first_params)
    acts = jnp.stack([first_out, second_out]).reshape(2, M, TOK_MB, MODEL_DIMENSION)
    dacts = jnp.stack([first_grad, second_grad]).reshape(2, M, TOK_MB, MODEL_DIMENSION)
    stacked = [jnp.stack([first_item, second_item]) for first_item, second_item in zip(first_grads, second_grads)]
    return (acts, dacts, stacked[0], stacked[1], stacked[2], stacked[3], stacked[4], stacked[5], stacked[6], stacked[7], stacked[8])
```

```python
import functools

import jax
import jax.numpy as jnp
from jax import lax
from jax.experimental import pallas as pl
from jax.experimental.pallas import tpu as pltpu
from jax.sharding import PartitionSpec as P

HEADS = 9
KV = 3
GROUP = HEADS // KV
HD = 64
KVW = KV * HD
QW = HEADS * HD
EPS = 1e-05
THETA = 100000.0
FLOOR = -1e30
BF = jnp.bfloat16
F32 = jnp.float32
VMEM_LIMIT = 62 * 1024 * 1024
MESH = pl.DeviceIdType.MESH
LANES = 128
N_SEMS = 280


def nt(a, b):
    return lax.dot_general(a, b, (((1,), (1,)), ((), ())), preferred_element_type=F32)


def tn(a, b):
    return lax.dot_general(a, b, (((0,), (0,)), ((), ())), preferred_element_type=F32)


def nn(a, b):
    return jnp.dot(a, b, preferred_element_type=F32)


def rope(t, cos, sa, sb):
    return t * cos + pltpu.roll(t, LANES - HD // 2, 1) * sa + pltpu.roll(t, HD // 2, 1) * sb


def rope_back(t, cos, sa, sb):
    return t * cos - pltpu.roll(t, LANES - HD // 2, 1) * sa - pltpu.roll(t, HD // 2, 1) * sb


class Shape:
    def __init__(self, sizes, inputs, w_q, w_gate):
        self.n_ctx, self.n_wt = sizes["ctx"], sizes["wt"]
        self.rows, self.width = inputs.shape[1], inputs.shape[2]
        self.near = self.n_wt // 2
        self.half = self.rows * self.near
        self.tokens = 2 * self.half
        self.block = 2 * self.half
        self.keys = 2 * self.n_ctx * self.block
        self.slice = w_q.shape[1]
        self.hidden = w_gate.shape[2]
        self.qkv = 2 * KVW + QW
        self.cols = self.qkv + self.width
        self.lead = -(-self.qkv // LANES) * LANES
        self.tail = self.qkv // LANES * LANES
        self.shift = self.qkv - self.tail
        self.last_start = self.keys - self.keys // 8 - 1
        self.keep = self.keys <= 4096


def kernel(z, *refs):
    (
        x_ref, cot_ref, cos_ref, sa_ref, sb_ref, pos_ref, doc_ref, ga_ref, gm_ref,
        wq_ref, wk_ref, wv_ref, wo_ref, gate_ref, up_ref, down_ref,
    ) = refs[:16]
    (
        acts_ref, dacts_ref, gga_ref, gwq_ref, gwk_ref, gwv_ref, gwo_ref, ggm_ref,
        ggate_ref, gup_ref, gdown_ref,
    ) = refs[16:27]
    (
        W, GU, DN, X, E, EB, GN, KVB, Q, O, LSE, R1, N2, R2, Z, G, UP, ACT, DG, DU, DO, DEL, DQ,
        DKV, SWAP, PILE, PM, PD, PA, RM, RD, RA, CM, CD, CA, GV, GT, GR, YA, YD, sem, turn,
    ) = refs[27:]
    n_ctx, n_wt, H, T, R = z.n_ctx, z.n_wt, z.half, z.tokens, z.block
    near = z.near
    s, c, w = lax.axis_index("section"), lax.axis_index("ctx"), lax.axis_index("wt")
    other = 1 - s
    partner = {"section": other}
    has_left, has_right = w > 0, w < n_wt - 1
    side, seat = lax.div(w, near), lax.rem(w, near)

    used = [0]
    pending = []

    def take(n=1):
        first = used[0]
        used[0] += n
        assert used[0] <= N_SEMS + 32 * n_ctx
        return first

    def when(cond, f):
        if cond is None:
            f()
        else:
            pl.when(cond)(lambda: (f(), None)[1])

    def remote(src, dst, si, ri, where):
        return pltpu.make_async_remote_copy(
            src_ref=src, dst_ref=dst, send_sem=sem.at[si], recv_sem=sem.at[ri],
            device_id=where, device_id_type=MESH,
        )

    def send(src, dst, si, ri, where, cond=None):
        copy = remote(src, dst, si, ri, where)
        when(cond, copy.start)
        pending.append((cond, copy.wait_send))

    def arrive(dst, ri, cond=None):
        when(cond, remote(dst, dst, ri, ri, partner).wait_recv)

    def flush():
        for cond, wait in pending:
            when(cond, wait)
        pending.clear()

    barrier = pltpu.get_barrier_semaphore()

    def greet(where):
        pl.semaphore_signal(barrier, inc=1, device_id=where, device_id_type=MESH)

    greet(partner)
    for d in range(1, n_wt):
        greet({"wt": lax.rem(w + d, n_wt)})
    for d in range(1, n_ctx):
        greet({"ctx": lax.rem(c + d, n_ctx)})

    load = [
        pltpu.make_async_copy(gate_ref.at[0], GU.at[s, w, 0], sem.at[take()]),
        pltpu.make_async_copy(up_ref.at[0], GU.at[s, w, 1], sem.at[take()]),
        pltpu.make_async_copy(down_ref.at[0], DN.at[s, w], sem.at[take()]),
    ]
    for copy in load:
        copy.start()
    first = pl.multiple_of(w * z.slice, 16)
    wk, wv = wk_ref[0], wv_ref[0]
    pieces = []
    for g in range(KV):
        pieces += [wk[:, g * HD : (g + 1) * HD], wv[:, g * HD : (g + 1) * HD]]
    W[s, pl.ds(first, z.slice), :] = jnp.concatenate(pieces + [wq_ref[0], wo_ref[0]], 1)
    GN[s, 0:1] = ga_ref[...]
    GN[s, 1:2] = gm_ref[...]
    EB[...] = cot_ref[...].astype(BF)

    pl.semaphore_wait(barrier, 1 + (n_wt - 1) + (n_ctx - 1))

    gain_send, gain_recv = take(), take()
    send(GN.at[s], GN.at[s], gain_send, gain_recv, partner)

    def rows_start(source, dest):
        sends, recvs = take(n_wt), take(n_wt)
        for d in range(1, n_wt):
            peer = lax.rem(w + d, n_wt)
            send(source, dest.at[seat], sends + peer, recvs + w, {"wt": peer}, side == s)
        return recvs

    def rows_end(dest, recvs):
        for i in range(near):
            k = s * near + i
            arrive(dest.at[i], recvs + k, k != w)

    half_ctx = n_ctx // 2
    bit_a, bit_b = lax.rem(c, 2), lax.rem(lax.div(c, half_ctx), 2)
    peer_a = {"ctx": c + 1 - 2 * bit_a}
    peer_b = {"ctx": c + half_ctx - 2 * half_ctx * bit_b}
    mine_q = (bit_a, 2 + bit_b)
    their_q = (1 - bit_a, 3 - bit_b)

    class Gather:
        def __init__(self, part, whole):
            self.part, self.whole = part, whole
            self.zr, self.right, self.left = take(2 * n_wt), take(2 * n_wt), take(2 * n_wt)
            self.xs, self.xr = take(2 * n_wt), take(2 * n_wt)
            self.ps, self.pr = take(n_wt), take(n_wt)

        def along(self, j, go_right, cond):
            base = self.right if go_right else self.left
            where = {"wt": w + 1 if go_right else w - 1}
            where = {"wt": lax.rem(where["wt"] + n_wt, n_wt)}
            for i in range(2):
                ref = self.part(s, j, mine_q[i])
                send(ref, ref, base + 2 * j + i, self.zr + 2 * j + i, where, cond)

        def over(self, j, cond=None):
            ref = self.whole(s, j)
            send(ref, ref, self.ps + j, self.pr + j, partner, cond)

        def start(self):
            self.along(w, True, has_right)
            self.along(w, False, has_left)
            self.over(w)

        def from_side(self, t):
            low = w - t
            high = w + t
            return (
                (lax.rem(low + n_wt, n_wt), low >= 0, True, has_right),
                (lax.rem(high, n_wt), high < n_wt, False, has_left),
            )

        def hop(self, t):
            for j, there, go_right, more in self.from_side(t):
                for i in range(2):
                    arrive(self.part(s, j, mine_q[i]), self.zr + 2 * j + i, there)
                self.along(j, go_right, there & more)
                for i, peer in enumerate((peer_a, peer_b)):
                    ref = self.part(s, j, mine_q[i])
                    send(ref, ref, self.xs + 2 * j + i, self.xr + 2 * j + i, peer, there)

        def cross(self, t):
            for j, there, go_right, more in self.from_side(t):
                for i in range(2):
                    arrive(self.part(s, j, their_q[i]), self.xr + 2 * j + i, there)
                self.over(j, there)

        def end(self):
            for j in range(n_wt):
                arrive(self.whole(other, j), self.pr + j)

    quarter = z.cols // 4
    g_w = Gather(
        lambda l, j, q: W.at[
            l, pl.ds(pl.multiple_of(j * z.slice, 16), z.slice),
            pl.ds(pl.multiple_of(q * quarter, LANES), quarter),
        ],
        lambda l, j: W.at[l, pl.ds(pl.multiple_of(j * z.slice, 16), z.slice)],
    )
    half_gu = z.width // 2
    g_gu = Gather(
        lambda l, j, q: GU.at[
            l, j, lax.div(q, 2), pl.ds(pl.multiple_of(lax.rem(q, 2) * half_gu, 16), half_gu)
        ],
        lambda l, j: GU.at[l, j],
    )
    quarter_d = z.hidden // 4
    g_dn = Gather(
        lambda l, j, q: DN.at[l, j, pl.ds(pl.multiple_of(q * quarter_d, 16), quarter_d)],
        lambda l, j: DN.at[l, j],
    )

    x_recv = rows_start(x_ref, X)
    g_w.start()
    own_x = pltpu.make_async_copy(x_ref, X.at[seat], sem.at[take()])
    own_e = pltpu.make_async_copy(EB, E.at[seat], sem.at[take()])
    when(side == s, own_x.start)
    when(side == s, own_e.start)
    for t in range(1, n_wt):
        g_w.hop(t)
    for copy in load:
        copy.wait()
    g_gu.start()
    g_dn.start()
    e_recv = rows_start(EB, E)
    for t in range(1, n_wt):
        g_w.cross(t)
    rows_end(X, x_recv)
    when(side == s, own_x.wait)
    arrive(GN.at[other], gain_recv)
    g_w.end()

    cos, sa, sb = cos_ref[...], sa_ref[...], sb_ref[...]
    lane = lax.broadcasted_iota(jnp.int32, (T, LANES), 1)
    is_key = lane < HD
    kcos = jnp.where(is_key, cos, 1.0)
    ksa, ksb = jnp.where(is_key, sa, 0.0), jnp.where(is_key, sb, 0.0)

    def rows_of(ref):
        return jnp.concatenate([ref[i, m] for m in range(2) for i in range(near)], 0)

    def store_rows(ref, value):
        for m in range(2):
            for i in range(near):
                at = m * H + i * z.rows
                ref[i, m] = value[at : at + z.rows]

    def head(value, h):
        return value[:, h * HD : (h + 1) * HD]

    q_tiles = -(-QW // LANES)

    def bounds(m):
        high = m * n_ctx + c
        start = high * R + s * H
        low = jnp.where(start >= z.last_start, z.last_start // R, 0)
        return low, high + 1

    def place_of(kb):
        return lax.rem(kb, n_ctx), lax.div(kb, n_ctx)

    def allowed(kb, m):
        at = kb * R + lax.broadcasted_iota(jnp.int32, (R, GROUP * H), 0)
        return (at <= pos_ref[m]) & (at >= doc_ref[m])

    def slot(l):
        return l if z.keep else 0

    def take_turn(i, near_too):
        for d in range(1, n_ctx):
            pl.semaphore_signal(
                turn.at[i], inc=1, device_id={"ctx": lax.rem(c + d, n_ctx)}, device_id_type=MESH
            )
        if near_too:
            pl.semaphore_signal(turn.at[i], inc=1, device_id=partner, device_id_type=MESH)
        pl.semaphore_wait(turn.at[i], n_ctx - 1 + int(near_too))

    def keys_of(l, g, cc, mm):
        return KVB[slot(l), g, cc, :, mm].reshape(R, LANES)

    def gather_kv(l):
        ks, kr = take(n_ctx + 1), take(n_ctx)
        fs, fr = take(n_ctx), take(n_ctx)
        ref = KVB.at[slot(l), :, c, s]
        for d in range(1, n_ctx):
            peer = lax.rem(c + d, n_ctx)
            send(ref, ref, ks + peer, kr + c, {"ctx": peer})
        send(ref, ref, ks + n_ctx, fr + c, partner)
        return kr, fs, fr

    def end_kv(l, sems):
        kr, fs, fr = sems
        for d in range(1, n_ctx):
            peer = lax.rem(c + n_ctx - d, n_ctx)
            ref = KVB.at[slot(l), :, peer, s]
            arrive(ref, kr + peer)
            send(ref, ref, fs + peer, fr + peer, partner)
        for peer in range(n_ctx):
            arrive(KVB.at[slot(l), :, peer, other], fr + peer)

    def store_kv(l, kvq):
        for g in range(KV):
            t = rope(kvq[:, g * LANES : (g + 1) * LANES], kcos, ksa, ksb).astype(BF)
            for m in range(2):
                KVB[slot(l), g, c, s, m] = t[m * H : (m + 1) * H]

    def attend(l):
        for m in range(2):

            def step(kb, carry, m=m):
                cc, mm = place_of(kb)
                ok = allowed(kb, m)
                out = []
                for g in range(KV):
                    top, total, acc = carry[3 * g : 3 * g + 3]
                    kv = keys_of(l, g, cc, mm)
                    sc = jnp.where(ok, nt(kv, Q[l, g, m]), FLOOR)
                    new = jnp.maximum(top, jnp.max(sc, 0, keepdims=True))
                    scale = jnp.exp(top - new)
                    p = jnp.exp(sc - new)
                    total = total * scale + jnp.sum(p, 0, keepdims=True)
                    acc = acc * scale + tn(kv, p.astype(BF))
                    out += [new, total, acc]
                return tuple(out)

            init = (
                jnp.full((1, GROUP * H), FLOOR, F32),
                jnp.zeros((1, GROUP * H), F32),
                jnp.zeros((LANES, GROUP * H), F32),
            )
            low, high = bounds(m)
            carry = lax.fori_loop(low, high, step, init * KV)
            for g in range(KV):
                top, total, acc = carry[3 * g : 3 * g + 3]
                out = jnp.transpose(acc[HD:] / total).astype(BF)
                for i in range(GROUP):
                    h = g * GROUP + i
                    O[l, m * H : (m + 1) * H, h * HD : (h + 1) * HD] = out[i * H : (i + 1) * H]
                LSE[l, g, m] = top + jnp.log(total)

    def forward(l, h, ready):
        ga, gm = GN[l, 0:1], GN[l, 1:2]
        r1 = lax.rsqrt(jnp.mean(h * h, -1, keepdims=True) + EPS)
        R1[l] = r1
        u = (h * r1 * ga).astype(BF)
        kvq = nn(u, W[l, :, : z.lead])
        if l == 1 and not z.keep:
            flush()
            take_turn(0, True)
        store_kv(l, kvq)
        sems = gather_kv(l)
        for i in range(q_tiles):
            at = KV * LANES + i * LANES
            t = rope(kvq[:, at : at + LANES], cos, sa, sb) * 0.125
            for k in range(LANES // HD):
                hd = i * (LANES // HD) + k
                if hd < HEADS:
                    moved = pltpu.roll(t, HD, 1) if k else t
                    moved = jnp.where(is_key, moved, 0.0).astype(BF)
                    g, at_h = hd // GROUP, hd % GROUP * H
                    for m in range(2):
                        Q[l, g, m, at_h : at_h + H] = moved[m * H : (m + 1) * H]
        end_kv(l, sems)
        attend(l)
        h2 = h + nn(O[l], W[l, :, z.tail :])[:, z.shift :]
        r2 = lax.rsqrt(jnp.mean(h2 * h2, -1, keepdims=True) + EPS)
        n2 = h2 * r2
        zz = (n2 * gm).astype(BF)
        R2[l] = r2
        N2[l] = n2
        Z[l] = zz
        ready()
        total = h2
        for j in range(n_wt):
            g = nn(zz, GU[l, j, 0])
            up = nn(zz, GU[l, j, 1])
            act = (g * jax.nn.sigmoid(g) * up).astype(BF)
            ACT[l, jnp.where(w == j, 0, 1)] = act
            if z.keep:
                G[l, j] = g
                UP[l, j] = up
            total = total + nn(act, DN[l, j])
        out = total.astype(BF)
        store_rows(YA.at[l], out)
        return out

    def mlp_ready():
        for t in range(1, n_wt):
            g_gu.hop(t)
            g_dn.hop(t)
        for t in range(1, n_wt):
            g_gu.cross(t)
            g_dn.cross(t)
        g_gu.end()
        g_dn.end()

    h0 = rows_of(X).astype(F32)
    mid = forward(0, h0, mlp_ready)
    forward(1, mid.astype(F32), lambda: None)

    rows_end(E, e_recv)
    when(side == s, own_e.wait)

    def give_rows(ref, out_ref):
        si, ri, li = take(), take(), take()
        send(ref.at[other, seat], out_ref.at[0], si, ri, partner, side == s)
        copy = pltpu.make_async_copy(ref.at[s, seat], out_ref.at[0], sem.at[li])
        when(side == s, copy.start)

        def end():
            when(side == s, copy.wait)
            arrive(out_ref.at[0], ri, side != s)

        return end

    acts_end = give_rows(YA, acts_ref)

    def column_slice(value):
        out = value[:, : z.slice]
        for j in range(1, n_wt):
            out = jnp.where(w == j, value[:, j * z.slice : (j + 1) * z.slice], out)
        return out

    def attend_back(l):
        DKV[...] = jnp.zeros(DKV.shape, BF)
        for m in range(2):

            def step(kb, carry, m=m):
                cc, mm = place_of(kb)
                ok = allowed(kb, m)
                out = []
                for g in range(KV):
                    dq = carry[g]
                    kv = keys_of(l, g, cc, mm)
                    q, do = Q[l, g, m], DO[g, m]
                    sc = jnp.where(ok, nt(kv, q), FLOOR)
                    p = jnp.exp(sc - LSE[l, g, m])
                    ds = (p * (nt(kv, do) - DEL[g, m])).astype(BF)
                    tile = nn(ds, q) + nn(p.astype(BF), do)
                    old = DKV[g, cc, :, mm].reshape(R, LANES).astype(F32)
                    DKV[g, cc, :, mm] = (old + tile).astype(BF).reshape(2, H, LANES)
                    out.append(dq + tn(kv, ds))
                return tuple(out)

            low, high = bounds(m)
            zero = jnp.zeros((LANES, GROUP * H), F32)
            carry = lax.fori_loop(low, high, step, (zero,) * KV)
            for g in range(KV):
                out = jnp.transpose(carry[g][:HD] * 0.125)
                for i in range(GROUP):
                    h = g * GROUP + i
                    DQ[m * H : (m + 1) * H, h * HD : (h + 1) * HD] = out[i * H : (i + 1) * H]

    def reduce_kv(l):
        if l == 0 and not z.keep:
            take_turn(2, True)
        ss, sr = take(), take()
        xs, xr = take(n_ctx), take(n_ctx)
        send(DKV.at[:, :, other], SWAP.at[slot(l)], ss, sr, partner)
        arrive(SWAP.at[slot(l)], sr)
        for g in range(KV):
            for cc in range(n_ctx):
                DKV[g, cc, s] = (DKV[g, cc, s].astype(F32) + SWAP[slot(l), g, cc].astype(F32)).astype(BF)
        for d in range(1, n_ctx):
            peer = lax.rem(c + d, n_ctx)
            send(DKV.at[:, peer, s], PILE.at[slot(l), c], xs + peer, xr + c, {"ctx": peer})
        PILE[slot(l), c] = DKV[:, c, s]
        for d in range(1, n_ctx):
            peer = lax.rem(c + n_ctx - d, n_ctx)
            arrive(PILE.at[slot(l), peer], xr + peer)
        out = []
        for g in range(KV):
            total = PILE[slot(l), 0, g].astype(F32)
            for cc in range(1, n_ctx):
                total = total + PILE[slot(l), cc, g].astype(F32)
            out.append(total.reshape(T, LANES))
        return out

    class Reduce:
        def __init__(self, part, got, cut, out):
            self.part, self.got, self.cut, self.out = part, got, cut, out
            self.ps, self.pr = take(), take()
            self.rs, self.rr, self.gs, self.gr = take(n_ctx), take(n_ctx), take(n_ctx), take(n_ctx)

        def give(self, l):
            send(self.part.at[l], self.got, self.ps, self.pr, partner, s != l)

        def scatter(self, l):
            arrive(self.got, self.pr, s == l)

            @pl.when(s == l)
            def _():
                for k in range(n_ctx):
                    both = self.part[l, k].astype(F32) + self.got[k].astype(F32)
                    self.part[l, k] = both.astype(BF)
                self.cut[c] = self.part[l, c]

            for d in range(1, n_ctx):
                peer = lax.rem(c + d, n_ctx)
                send(
                    self.part.at[l, peer], self.cut.at[c], self.rs + peer, self.rr + c,
                    {"ctx": peer}, s == l,
                )

        def gather(self, l):
            for d in range(1, n_ctx):
                peer = lax.rem(c + n_ctx - d, n_ctx)
                arrive(self.cut.at[peer], self.rr + peer, s == l)

            @pl.when(s == l)
            def _():
                total = self.cut[0].astype(F32)
                for cc in range(1, n_ctx):
                    total = total + self.cut[cc].astype(F32)
                self.out[c] = total.astype(BF)

            for d in range(1, n_ctx):
                peer = lax.rem(c + d, n_ctx)
                ref = self.out.at[c]
                send(ref, ref, self.gs + peer, self.gr + c, {"ctx": peer}, s == l)

        def end(self):
            for d in range(1, n_ctx):
                peer = lax.rem(c + n_ctx - d, n_ctx)
                arrive(self.out.at[peer], self.gr + peer)

    red_m = Reduce(PM, RM, CM, RM)
    red_d = Reduce(PD, RD, CD, RD)
    red_a = Reduce(PA, RA, CA, RA)

    def backward(l, e, h, after_mlp, after_attention):
        ga, gm = GN[l, 0:1], GN[l, 1:2]
        eb = e.astype(BF)
        zz = Z[l]
        dz = jnp.zeros((T, z.width), F32)
        for j in range(n_wt):
            da = nt(eb, DN[l, j])
            if z.keep:
                g, up = G[l, j], UP[l, j]
            else:
                g, up = nn(zz, GU[l, j, 0]), nn(zz, GU[l, j, 1])
            sg = jax.nn.sigmoid(g)
            dg = (da * up * sg * (1.0 + g * (1.0 - sg))).astype(BF)
            du = (da * g * sg).astype(BF)
            kept = jnp.where(w == j, 0, 1)
            DG[kept] = dg
            DU[kept] = du
            dz = dz + nt(dg, GU[l, j, 0]) + nt(du, GU[l, j, 1])
        n2, r2 = N2[l], R2[l]
        m2 = dz * gm
        dh2 = e + r2 * (m2 - n2 * jnp.mean(m2 * n2, -1, keepdims=True))
        ob = dh2.astype(BF)
        wide = jnp.concatenate([jnp.zeros((T, z.shift), BF), ob], 1) if z.shift else ob
        do = nt(wide, W[l, :, z.tail :]).astype(BF)
        o = O[l]
        prod = do.astype(F32) * o.astype(F32)
        blank = jnp.zeros((T, HD), BF)
        for h_i in range(HEADS):
            t = jnp.concatenate([blank, head(do, h_i)], 1)
            g, at = h_i // GROUP, h_i % GROUP * H
            for m in range(2):
                DO[g, m, at : at + H] = t[m * H : (m + 1) * H]
        for g in range(KV):
            for m in range(2):
                stacked = jnp.concatenate(
                    [head(prod, g * GROUP + i)[m * H : (m + 1) * H] for i in range(GROUP)], 0
                )
                DEL[g, m] = jnp.sum(jnp.transpose(stacked), 0, keepdims=True)

        gg, gu = tn(zz, DG[0]), tn(zz, DU[0])
        gd = tn(ACT[l, 0], eb)
        mine = 2 * z.width // n_ctx
        for k in range(n_ctx):
            both = jnp.concatenate([gg, gu], 0)[k * mine : (k + 1) * mine]
            PM[l, k] = both.astype(BF)
            low = z.hidden // n_ctx
            PD[l, k] = gd[k * low : (k + 1) * low].astype(BF)
        after_mlp()
        if l == 0 and not z.keep:
            flush()
            take_turn(1, True)
            u = (h * R1[l] * ga).astype(BF)
            store_kv(l, nn(u, W[l, :, : KV * LANES]))
            end_kv(l, gather_kv(l))
        attend_back(l)
        after_attention()
        dkv = reduce_kv(l)
        parts = [rope_back(dkv[g], kcos, ksa, ksb).astype(BF) for g in range(KV)]
        for i in range(q_tiles):
            at = i * LANES
            t = rope_back(DQ[:, at : at + LANES], cos, sa, sb)
            if at + LANES > QW:
                t = jnp.where(is_key, t, 0.0)
            parts.append(t.astype(BF))
        dqkv = jnp.concatenate(parts, 1)
        n1 = h * R1[l]
        u = (n1 * ga).astype(BF)
        du_in = nt(dqkv, W[l, :, : z.lead])
        m1 = du_in * ga
        e_next = (dh2 + R1[l] * (m1 - n1 * jnp.mean(m1 * n1, -1, keepdims=True))).astype(BF)
        store_rows(YD.at[l], e_next)
        g_a = tn(column_slice(u), dqkv)[:, : z.qkv]
        g_o = tn(column_slice(o), ob)
        g_a = jnp.concatenate([g_a, g_o], 1)
        wide_a = z.cols // n_ctx
        for k in range(n_ctx):
            PA[l, k] = g_a[:, k * wide_a : (k + 1) * wide_a].astype(BF)
        GV[l, 0:1] = jnp.sum(du_in * n1, 0, keepdims=True)
        GV[l, 1:2] = jnp.sum(dz * n2, 0, keepdims=True)
        return e_next

    def after_mlp_1():
        red_m.give(1)
        red_d.give(1)

    def after_attention_1():
        red_m.scatter(1)
        red_d.scatter(1)

    def after_mlp_0():
        red_m.give(0)
        red_d.give(0)
        red_a.scatter(1)
        red_m.gather(1)
        red_d.gather(1)

    def after_attention_0():
        red_a.gather(1)
        red_m.scatter(0)
        red_d.scatter(0)

    e1 = rows_of(E).astype(F32)
    e0 = backward(1, e1, mid.astype(F32), after_mlp_1, after_attention_1)
    red_a.give(1)
    flush()
    backward(0, e0.astype(F32), h0, after_mlp_0, after_attention_0)
    red_a.give(0)
    gp, gq, gx, gy = take(), take(), take(n_ctx), take(n_ctx)
    send(GV.at[other], GT, gp, gq, partner)
    dacts_end = give_rows(YD, dacts_ref)
    red_m.gather(0)
    red_d.gather(0)
    red_a.scatter(0)
    arrive(GT, gq)
    GR[c] = GV[s] + GT[...]
    for d in range(1, n_ctx):
        peer = lax.rem(c + d, n_ctx)
        send(GR.at[c], GR.at[c], gx + peer, gy + c, {"ctx": peer})
    red_a.gather(0)
    red_m.end()
    red_d.end()
    per = n_ctx // 2
    mine = 2 * z.width // n_ctx
    for k in range(per):
        ggate_ref[0, k * mine : (k + 1) * mine] = RM[k].astype(F32)
        gup_ref[0, k * mine : (k + 1) * mine] = RM[per + k].astype(F32)
    low = z.hidden // n_ctx
    for k in range(n_ctx):
        gdown_ref[0, k * low : (k + 1) * low] = RD[k].astype(F32)
    for d in range(1, n_ctx):
        peer = lax.rem(c + n_ctx - d, n_ctx)
        arrive(GR.at[peer], gy + peer)
    gain = GR[0]
    for cc in range(1, n_ctx):
        gain = gain + GR[cc]
    gain = column_slice(gain)
    gga_ref[...] = gain[0:1]
    ggm_ref[...] = gain[1:2]
    red_a.end()
    total = jnp.concatenate([RA[k] for k in range(n_ctx)], 1).astype(F32)
    for g in range(KV):
        at = g * LANES
        gwk_ref[0, :, g * HD : (g + 1) * HD] = total[:, at : at + HD]
        gwv_ref[0, :, g * HD : (g + 1) * HD] = total[:, at + HD : at + LANES]
    gwq_ref[0] = total[:, 2 * KVW : z.qkv]
    gwo_ref[0] = total[:, z.qkv :]
    acts_end()
    dacts_end()
    flush()


def local(
    sizes, inputs, doc_start, attn_gain, w_q, w_k, w_v, w_o, mlp_gain, w_gate, w_up, w_down,
    cotangent,
):
    z = Shape(sizes, inputs, w_q, w_gate)
    n_ctx, n_wt, H, T, R = z.n_ctx, z.n_wt, z.half, z.tokens, z.block
    near, D, F, rows = z.near, z.width, z.hidden, z.rows
    s, c = lax.axis_index("section"), lax.axis_index("ctx")
    first = c * R + s * H
    doc = lax.dynamic_slice(doc_start, (0, first), (2, H))
    pos = first + jnp.arange(2, dtype=jnp.int32)[:, None] * (n_ctx * R)
    pos = pos + jnp.arange(H, dtype=jnp.int32)[None, :]
    half = HD // 2
    inverse = 1.0 / THETA ** (jnp.arange(half).astype(F32) * 2.0 / HD)
    angles = (pos - doc).astype(F32).reshape(T)[:, None] * inverse[None, :]
    cos, sin = jnp.cos(angles), jnp.sin(angles)
    nil = jnp.zeros_like(sin)
    cos = jnp.concatenate([cos] * 4, 1)
    sa = jnp.concatenate([-sin, nil] * 2, 1)
    sb = jnp.concatenate([nil, sin] * 2, 1)
    pos_row = jnp.tile(pos, (1, GROUP))[:, None]
    doc_row = jnp.tile(doc, (1, GROUP))[:, None]

    vm = pl.BlockSpec(memory_space=pltpu.VMEM)
    hbm = pl.BlockSpec(memory_space=pl.ANY)
    shape = jax.ShapeDtypeStruct
    outs = [
        shape((1, 2, rows, D), BF), shape((1, 2, rows, D), BF), shape((1, z.slice), F32),
        shape((1, z.slice, QW), F32), shape((1, z.slice, KVW), F32),
        shape((1, z.slice, KVW), F32), shape((1, z.slice, D), F32), shape((1, z.slice), F32),
        shape((1, D, F), F32), shape((1, D, F), F32), shape((1, F, D), F32),
    ]
    layers = 2 if z.keep else 1
    keep = (n_wt, T, F) if z.keep else (1, 8, LANES)
    big, small, thin = 2 * D // n_ctx, F // n_ctx, z.cols // n_ctx
    vmem = pltpu.VMEM
    scratch = [
        vmem((2, n_wt * z.slice, z.cols), BF),
        vmem((2, n_wt, 2, D, F), BF),
        vmem((2, n_wt, F, D), BF),
        vmem((near, 2, rows, D), BF),
        vmem((near, 2, rows, D), BF),
        vmem((2, rows, D), BF),
        vmem((2, 8, D), F32),
        vmem((layers, KV, n_ctx, 2, 2, H, LANES), BF),
        vmem((2, KV, 2, GROUP * H, LANES), BF),
        vmem((2, T, QW), BF),
        vmem((2, KV, 2, 1, GROUP * H), F32),
        vmem((2, T, 1), F32),
        vmem((2, T, D), F32),
        vmem((2, T, 1), F32),
        vmem((2, T, D), BF),
        vmem((2,) + keep, F32),
        vmem((2,) + keep, F32),
        vmem((2, 2, T, F), BF),
        vmem((2, T, F), BF),
        vmem((2, T, F), BF),
        vmem((KV, 2, GROUP * H, LANES), BF),
        vmem((KV, 2, 1, GROUP * H), F32),
        vmem((T, -(-QW // LANES) * LANES), F32),
        vmem((KV, n_ctx, 2, 2, H, LANES), BF),
        vmem((layers, KV, n_ctx, 2, H, LANES), BF),
        vmem((layers, n_ctx, KV, 2, H, LANES), BF),
        vmem((2, n_ctx, big, F), BF),
        vmem((2, n_ctx, small, D), BF),
        vmem((2, n_ctx, z.slice, thin), BF),
        vmem((n_ctx, big, F), BF),
        vmem((n_ctx, small, D), BF),
        vmem((n_ctx, z.slice, thin), BF),
        vmem((n_ctx, big, F), BF),
        vmem((n_ctx, small, D), BF),
        vmem((n_ctx, z.slice, thin), BF),
        vmem((2, 8, D), F32),
        vmem((8, D), F32),
        vmem((n_ctx, 8, D), F32),
        vmem((2, near, 2, rows, D), BF),
        vmem((2, near, 2, rows, D), BF),
        pltpu.SemaphoreType.DMA((N_SEMS + 32 * n_ctx,)),
        pltpu.SemaphoreType.REGULAR((4,)),
    ]
    return pl.pallas_call(
        functools.partial(kernel, z),
        out_shape=outs,
        in_specs=[vm] * 13 + [hbm] * 3,
        out_specs=[vm] * 11,
        scratch_shapes=scratch,
        compiler_params=pltpu.CompilerParams(
            collective_id=0, has_side_effects=True, vmem_limit_bytes=VMEM_LIMIT
        ),
        name="step",
    )(
        inputs, cotangent, cos, sa, sb, pos_row, doc_row, attn_gain, mlp_gain,
        w_q, w_k, w_v, w_o, w_gate, w_up, w_down,
    )


def solution(mesh):
    in_specs = (
        P(None, ("ctx", "wt"), None),
        P(),
        P("section", None),
        P("section", "wt", None),
        P("section", "wt", None),
        P("section", "wt", None),
        P("section", "wt", None),
        P("section", None),
        P("section", None, "wt"),
        P("section", None, "wt"),
        P("section", "wt", None),
        P(None, ("ctx", "wt"), None),
    )
    out_specs = (
        P("section", None, ("ctx", "wt"), None),
        P("section", None, ("ctx", "wt"), None),
        P("section", "wt"),
        P("section", "wt", None),
        P("section", "wt", None),
        P("section", "wt", None),
        P("section", "wt", None),
        P("section", "wt"),
        P("section", None, "wt"),
        P("section", None, "wt"),
        P("section", "wt", None),
    )
    sizes = dict(mesh.shape)
    return jax.shard_map(
        functools.partial(local, sizes), mesh=mesh, in_specs=in_specs, out_specs=out_specs,
        check_vma=False,
    )
```

```python
import functools

import jax
import jax.numpy as jnp
import numpy as np
from jax import lax
from jax.experimental import pallas as pl
from jax.experimental.pallas import tpu as pltpu
from jax.sharding import PartitionSpec as P

HEADS = 9
KV = 3
GROUP = HEADS // KV
HD = 64
KVW = KV * HD
QW = HEADS * HD
EPS = 1e-05
THETA = 100000.0
FLOOR = -1e30
BF = jnp.bfloat16
F32 = jnp.float32
VMEM_LIMIT = 62 * 1024 * 1024
MESH = pl.DeviceIdType.MESH
LANES = 128
N_SEMS = 280


def nt(a, b):
    return lax.dot_general(a, b, (((1,), (1,)), ((), ())), preferred_element_type=F32)


def tn(a, b):
    return lax.dot_general(a, b, (((0,), (0,)), ((), ())), preferred_element_type=F32)


def nn(a, b):
    return jnp.dot(a, b, preferred_element_type=F32)


def rope(t, cos, sa, sb):
    return t * cos + pltpu.roll(t, LANES - HD // 2, 1) * sa + pltpu.roll(t, HD // 2, 1) * sb


def rope_back(t, cos, sa, sb):
    return t * cos - pltpu.roll(t, LANES - HD // 2, 1) * sa - pltpu.roll(t, HD // 2, 1) * sb


class Shape:
    def __init__(self, sizes, inputs, w_q, w_gate):
        self.n_ctx, self.n_wt = sizes["ctx"], sizes["wt"]
        self.rows, self.width = inputs.shape[1], inputs.shape[2]
        self.near = self.n_wt // 2
        self.half = self.rows * self.near
        self.tokens = 2 * self.half
        self.block = 2 * self.half
        self.keys = 2 * self.n_ctx * self.block
        self.slice = w_q.shape[1]
        self.hidden = w_gate.shape[2]
        self.qkv = 2 * KVW + QW
        self.cols = self.qkv + self.width
        self.lead = -(-self.qkv // LANES) * LANES
        self.tail = self.qkv // LANES * LANES
        self.shift = self.qkv - self.tail
        self.last_start = self.keys - self.keys // 8 - 1
        self.keep = self.keys <= 4096


def kernel(z, *refs):
    (
        x_ref, cot_ref, start_ref, freq_ref, ga_ref, gm_ref, wq_ref, wk_ref, wv_ref, wo_ref,
        gate_ref, up_ref, down_ref,
    ) = refs[:13]
    acts_ref, dacts_ref, RM, RO, RA, gain_ref = refs[13:19]
    (
        W, MW, X, E, EB, GN, KVB, Q, O, LSE, R1, N2, R2, Z, G, UP, ACT, DG, DU, DO, DEL, DQ,
        DKV, DKO, SWAP, PILE, PM, PO, PA, CM, CO, CA, GV, GT, GR, YA, YD, POS, DOC, sem, turn,
    ) = refs[19:]
    n_ctx, n_wt, H, T, R = z.n_ctx, z.n_wt, z.half, z.tokens, z.block
    near = z.near
    s, c, w = lax.axis_index("section"), lax.axis_index("ctx"), lax.axis_index("wt")
    other = 1 - s
    partner = {"section": other}
    has_left, has_right = w > 0, w < n_wt - 1
    side, seat = lax.div(w, near), lax.rem(w, near)

    used = [0]
    pending = []

    def take(n=1):
        first = used[0]
        used[0] += n
        assert used[0] <= N_SEMS + 56 * n_ctx
        return first

    def when(cond, f):
        if cond is None:
            f()
        else:
            pl.when(cond)(lambda: (f(), None)[1])

    def remote(src, dst, si, ri, where):
        return pltpu.make_async_remote_copy(
            src_ref=src, dst_ref=dst, send_sem=sem.at[si], recv_sem=sem.at[ri],
            device_id=where, device_id_type=MESH,
        )

    def send(src, dst, si, ri, where, cond=None, out=pending):
        copy = remote(src, dst, si, ri, where)
        when(cond, copy.start)
        out.append((cond, copy.wait_send))

    def arrive(dst, ri, cond=None):
        when(cond, remote(dst, dst, ri, ri, partner).wait_recv)

    def flush(out=pending):
        for cond, wait in out:
            when(cond, wait)
        out.clear()

    barrier = pltpu.get_barrier_semaphore()

    def greet(where):
        pl.semaphore_signal(barrier, inc=1, device_id=where, device_id_type=MESH)

    greet(partner)
    for d in range(1, n_wt):
        greet({"wt": lax.rem(w + d, n_wt)})
    for d in range(1, n_ctx):
        greet({"ctx": lax.rem(c + d, n_ctx)})

    D = z.width
    load = [
        pltpu.make_async_copy(ref.at[0], MW.at[s, w, pl.ds(i * D, D)], sem.at[take()])
        for i, ref in enumerate((gate_ref, up_ref, down_ref))
    ]
    for copy in load:
        copy.start()
    first = pl.multiple_of(w * z.slice, 16)
    wk, wv = wk_ref[0], wv_ref[0]
    pieces = []
    for g in range(KV):
        pieces += [wk[:, g * HD : (g + 1) * HD], wv[:, g * HD : (g + 1) * HD]]
    W[s, pl.ds(first, z.slice), :] = jnp.concatenate(pieces + [wq_ref[0], wo_ref[0]], 1)
    GN[s, 0:1] = ga_ref[...]
    GN[s, 1:2] = gm_ref[...]
    pl.semaphore_wait(barrier, 1 + (n_wt - 1) + (n_ctx - 1))

    gain_send, gain_recv = take(), take()
    send(GN.at[s], GN.at[s], gain_send, gain_recv, partner)

    def rows_start(source, dest):
        sends, recvs = take(n_wt), take(n_wt)
        for d in range(1, n_wt):
            peer = lax.rem(w + d, n_wt)
            send(source, dest.at[seat], sends + peer, recvs + w, {"wt": peer}, side == s)
        return recvs

    def rows_end(dest, recvs):
        for i in range(near):
            k = s * near + i
            arrive(dest.at[i], recvs + k, k != w)

    half_ctx = n_ctx // 2
    bit_a, bit_b = lax.rem(c, 2), lax.rem(lax.div(c, half_ctx), 2)
    peer_a = {"ctx": c + 1 - 2 * bit_a}
    peer_b = {"ctx": c + half_ctx - 2 * half_ctx * bit_b}
    mine_q = (bit_a, 2 + bit_b)
    their_q = (1 - bit_a, 3 - bit_b)

    class Gather:
        def __init__(self, part, whole):
            self.part, self.whole = part, whole
            self.zr, self.right, self.left = take(2 * n_wt), take(2 * n_wt), take(2 * n_wt)
            self.xs, self.xr = take(2 * n_wt), take(2 * n_wt)
            self.ps, self.pr = take(n_wt), take(n_wt)

        def along(self, j, go_right, cond):
            base = self.right if go_right else self.left
            where = {"wt": lax.rem(w + 1 if go_right else w + n_wt - 1, n_wt)}
            for i in range(2):
                ref = self.part(s, j, mine_q[i])
                send(ref, ref, base + 2 * j + i, self.zr + 2 * j + i, where, cond)

        def over(self, j, cond):
            ref = self.whole(s, j)
            send(ref, ref, self.ps + j, self.pr + j, partner, cond)

        def start(self, l):
            self.along(w, True, (s == l) & has_right)
            self.along(w, False, (s == l) & has_left)
            self.over(w, s == l)

        def from_side(self, l, t):
            low, high = w - t, w + t
            return (
                (lax.rem(low + n_wt, n_wt), (s == l) & (low >= 0), True, has_right),
                (lax.rem(high, n_wt), (s == l) & (high < n_wt), False, has_left),
            )

        def hop(self, l, t):
            for j, there, go_right, more in self.from_side(l, t):
                for i in range(2):
                    arrive(self.part(s, j, mine_q[i]), self.zr + 2 * j + i, there)
                if t < n_wt - 1:
                    self.along(j, go_right, there & more)
                for i, peer in enumerate((peer_a, peer_b)):
                    ref = self.part(s, j, mine_q[i])
                    send(ref, ref, self.xs + 2 * j + i, self.xr + 2 * j + i, peer, there)

        def cross(self, l, t):
            for j, there, go_right, more in self.from_side(l, t):
                for i in range(2):
                    arrive(self.part(s, j, their_q[i]), self.xr + 2 * j + i, there)
                self.over(j, there)

        def end(self, l):
            for j in range(n_wt):
                arrive(self.whole(other, j), self.pr + j, s != l)

    quarter = z.cols // 4
    g_w = Gather(
        lambda l, j, q: W.at[
            l, pl.ds(pl.multiple_of(j * z.slice, 16), z.slice),
            pl.ds(pl.multiple_of(q * quarter, LANES), quarter),
        ],
        lambda l, j: W.at[l, pl.ds(pl.multiple_of(j * z.slice, 16), z.slice)],
    )
    quarter_m = 3 * D // 4
    g_m = Gather(
        lambda l, j, q: MW.at[l, j, pl.ds(pl.multiple_of(q * quarter_m, 16), quarter_m)],
        lambda l, j: MW.at[l, j],
    )

    x_recv = rows_start(x_ref, X)
    g_w.start(0)
    own_x = pltpu.make_async_copy(x_ref, X.at[seat], sem.at[take()])
    when(side == s, own_x.start)

    lane = lax.broadcasted_iota(jnp.int32, (T, LANES), 1)
    is_key = lane < HD
    angles = []
    for m in range(2):
        at = c * R + s * H
        doc = start_ref[m : m + 1, pl.ds(pl.multiple_of(at, LANES), H)]
        pos = m * n_ctx * R + at + lax.broadcasted_iota(jnp.int32, (1, H), 1)
        POS[m] = jnp.concatenate([pos] * GROUP, 1)
        DOC[m] = jnp.concatenate([doc] * GROUP, 1)
        gap = jnp.broadcast_to((pos - doc).astype(F32), (LANES, H))
        angles.append(jnp.transpose(gap) * freq_ref[...])
    angles = jnp.concatenate(angles, 0)
    cos, sin = jnp.cos(angles), jnp.sin(angles)
    first_half = lax.rem(lane, HD) < HD // 2
    sa, sb = jnp.where(first_half, -sin, 0.0), jnp.where(first_half, 0.0, sin)
    kcos = jnp.where(is_key, cos, 1.0)
    ksa, ksb = jnp.where(is_key, sa, 0.0), jnp.where(is_key, sb, 0.0)
    EB[...] = cot_ref[...].astype(BF)

    for copy in load:
        copy.wait()
    for t in range(1, n_wt):
        g_w.hop(0, t)
    g_m.start(0)
    for t in range(1, n_wt):
        g_w.cross(0, t)
    rows_end(X, x_recv)
    when(side == s, own_x.wait)
    arrive(GN.at[other], gain_recv)
    g_w.end(0)

    def rows_of(ref):
        return jnp.concatenate([ref[i, m] for m in range(2) for i in range(near)], 0)

    def store_rows(ref, value):
        for m in range(2):
            for i in range(near):
                at = m * H + i * z.rows
                ref[i, m] = value[at : at + z.rows]

    def head(value, h):
        return value[:, h * HD : (h + 1) * HD]

    q_tiles = -(-QW // LANES)

    def bounds(m):
        high = m * n_ctx + c
        start = high * R + s * H
        low = jnp.where(start >= z.last_start, z.last_start // R, 0)
        return low, high + 1

    def place_of(kb):
        return lax.rem(kb, n_ctx), lax.div(kb, n_ctx)

    def allowed(kb, m):
        at = kb * R + lax.broadcasted_iota(jnp.int32, (R, GROUP * H), 0)
        return (at <= POS[m]) & (at >= DOC[m])

    def slot(l):
        return l if z.keep else 0

    def take_turn(i, near_too):
        for d in range(1, n_ctx):
            pl.semaphore_signal(
                turn.at[i], inc=1, device_id={"ctx": lax.rem(c + d, n_ctx)}, device_id_type=MESH
            )
        if near_too:
            pl.semaphore_signal(turn.at[i], inc=1, device_id=partner, device_id_type=MESH)
        pl.semaphore_wait(turn.at[i], n_ctx - 1 + int(near_too))

    def keys_of(l, g, cc, mm):
        return KVB[slot(l), g, cc, :, mm].reshape(R, LANES)

    def gather_kv(l):
        out = []
        for m in range(2):
            ks, kr, fs, fr = take(n_ctx + 1), take(n_ctx), take(n_ctx), take(n_ctx)
            ref = KVB.at[slot(l), :, c, s, m]
            send(ref, ref, ks + n_ctx, fr + c, partner)
            for d in range(1, n_ctx):
                peer = lax.rem(c + d, n_ctx)
                send(ref, ref, ks + peer, kr + c, {"ctx": peer}, None if m == 0 else peer > c)
            out.append((kr, fs, fr))
        return out

    def end_kv(l, m, sems):
        kr, fs, fr = sems[m]
        peers = [lax.rem(c + n_ctx - d, n_ctx) for d in range(1, n_ctx)]
        for peer in peers:
            there = None if m == 0 else peer < c
            ref = KVB.at[slot(l), :, peer, s, m]
            arrive(ref, kr + peer, there)
            send(ref, ref, fs + peer, fr + peer, partner, there)
        arrive(KVB.at[slot(l), :, c, other, m], fr + c)
        for peer in peers:
            there = None if m == 0 else peer < c
            arrive(KVB.at[slot(l), :, peer, other, m], fr + peer, there)

    def store_kv(l, kvq):
        for g in range(KV):
            t = rope(kvq[:, g * LANES : (g + 1) * LANES], kcos, ksa, ksb).astype(BF)
            for m in range(2):
                KVB[slot(l), g, c, s, m] = t[m * H : (m + 1) * H]

    def attend(l, m, loop, carry):
        def step(kb, carry):
            cc, mm = place_of(kb)
            ok = allowed(kb, m)
            out = []
            for g in range(KV):
                top, total, acc = carry[3 * g : 3 * g + 3]
                kv = keys_of(l, g, cc, mm)
                sc = jnp.where(ok, nt(kv, Q[l, g, m]), FLOOR)
                new = jnp.maximum(top, jnp.max(sc, 0, keepdims=True))
                scale = jnp.exp(top - new)
                p = jnp.exp(sc - new)
                total = total * scale + jnp.sum(p, 0, keepdims=True)
                acc = acc * scale + tn(kv, p.astype(BF))
                out += [new, total, acc]
            return tuple(out)

        if carry is None:
            carry = (
                jnp.full((1, GROUP * H), FLOOR, F32),
                jnp.zeros((1, GROUP * H), F32),
                jnp.zeros((LANES, GROUP * H), F32),
            ) * KV
        return lax.fori_loop(*loop, step, carry)

    def attended(l, m, carry):
        for g in range(KV):
            top, total, acc = carry[3 * g : 3 * g + 3]
            out = jnp.transpose(acc[HD:] / total).astype(BF)
            for i in range(GROUP):
                h = g * GROUP + i
                O[l, m * H : (m + 1) * H, h * HD : (h + 1) * HD] = out[i * H : (i + 1) * H]
            LSE[l, g, m] = top + jnp.log(total)

    def forward(l, h, hook):
        ga, gm = GN[l, 0:1], GN[l, 1:2]
        r1 = lax.rsqrt(jnp.mean(h * h, -1, keepdims=True) + EPS)
        R1[l] = r1
        u = (h * r1 * ga).astype(BF)
        kvq = nn(u, W[l, :, : z.lead])
        if l == 1 and not z.keep:
            flush()
            take_turn(0, True)
        store_kv(l, kvq)
        sems = gather_kv(l)
        for i in range(q_tiles):
            at = KV * LANES + i * LANES
            t = rope(kvq[:, at : at + LANES], cos, sa, sb) * 0.125
            for k in range(LANES // HD):
                hd = i * (LANES // HD) + k
                if hd < HEADS:
                    moved = pltpu.roll(t, HD, 1) if k else t
                    moved = jnp.where(is_key, moved, 0.0).astype(BF)
                    g, at_h = hd // GROUP, hd % GROUP * H
                    for m in range(2):
                        Q[l, g, m, at_h : at_h + H] = moved[m * H : (m + 1) * H]
        end_kv(l, 0, sems)
        hook[0]()
        attended(l, 0, attend(l, 0, bounds(0), None))
        low, high = bounds(1)
        split = jnp.maximum(low, n_ctx)
        carry = attend(l, 1, (low, split), None)
        end_kv(l, 1, sems)
        hook[1]()
        attended(l, 1, attend(l, 1, (split, high), carry))
        hook[2]()
        h2 = h + nn(O[l], W[l, :, z.tail :])[:, z.shift :]
        r2 = lax.rsqrt(jnp.mean(h2 * h2, -1, keepdims=True) + EPS)
        n2 = h2 * r2
        zz = (n2 * gm).astype(BF)
        R2[l] = r2
        N2[l] = n2
        Z[l] = zz
        hook[3]()
        total = h2
        for k in range(n_wt):
            j = lax.rem(w + k, n_wt)
            g = nn(zz, MW[l, j, :D])
            up = nn(zz, MW[l, j, D : 2 * D])
            act = (g * jax.nn.sigmoid(g) * up).astype(BF)
            if k == 0:
                ACT[l] = act
            if z.keep:
                G[l, k] = g
                UP[l, k] = up
            total = total + nt(act, MW[l, j, 2 * D :])
        out = total.astype(BF)
        store_rows(YA.at[l], out)
        return out

    def first_0():
        g_m.hop(0, 1)
        g_w.start(1)

    def first_1():
        g_m.hop(0, 2)
        g_m.cross(0, 1)
        g_w.hop(1, 1)

    def first_2():
        g_m.hop(0, 3)
        g_m.cross(0, 2)
        g_w.hop(1, 2)
        g_w.cross(1, 1)

    def first_3():
        g_w.hop(1, 3)
        g_w.cross(1, 2)
        g_m.start(1)
        g_m.cross(0, 3)
        g_m.end(0)

    def second_0():
        g_m.hop(1, 1)

    def second_1():
        g_m.hop(1, 2)
        g_m.cross(1, 1)

    def second_2():
        g_m.hop(1, 3)
        g_m.cross(1, 2)

    def second_3():
        g_m.cross(1, 3)
        g_m.end(1)

    h0 = rows_of(X).astype(F32)
    mid = forward(0, h0, (first_0, first_1, first_2, first_3))
    g_w.cross(1, 3)
    e_recv = rows_start(EB, E)
    own_e = pltpu.make_async_copy(EB, E.at[seat], sem.at[take()])
    when(side == s, own_e.start)
    g_w.end(1)
    forward(1, mid.astype(F32), (second_0, second_1, second_2, second_3))

    rows_end(E, e_recv)
    when(side == s, own_e.wait)

    def give_rows(ref, out_ref):
        si, ri, li = take(), take(), take()
        send(ref.at[other, seat], out_ref, si, ri, partner, side == s)
        copy = pltpu.make_async_copy(ref.at[s, seat], out_ref, sem.at[li])
        when(side == s, copy.start)

        def end():
            when(side == s, copy.wait)
            arrive(out_ref, ri, side != s)

        return end

    acts_end = give_rows(YA, acts_ref)

    def column_slice(value):
        out = value[:, : z.slice]
        for j in range(1, n_wt):
            out = jnp.where(w == j, value[:, j * z.slice : (j + 1) * z.slice], out)
        return out

    kv_pending = []

    def attend_back(l, m, loop, carry):
        def step(kb, carry):
            cc, mm = place_of(kb)
            ok = allowed(kb, m)
            out = []
            for g in range(KV):
                dq = carry[g]
                kv = keys_of(l, g, cc, mm)
                q, do = Q[l, g, m], DO[g, m]
                sc = jnp.where(ok, nt(kv, q), FLOOR)
                p = jnp.exp(sc - LSE[l, g, m])
                ds = (p * (nt(kv, do) - DEL[g, m])).astype(BF)
                tile = nn(ds, q) + nn(p.astype(BF), do)
                old = DKV[g, cc, :, mm].reshape(R, LANES).astype(F32)
                DKV[g, cc, :, mm] = (old + tile).astype(BF).reshape(2, H, LANES)
                out.append(dq + tn(kv, ds))
            return tuple(out)

        if carry is None:
            carry = (jnp.zeros((LANES, GROUP * H), F32),) * KV
        return lax.fori_loop(*loop, step, carry)

    def attended_back(m, carry):
        for g in range(KV):
            out = jnp.transpose(carry[g][:HD] * 0.125)
            for i in range(GROUP):
                h = g * GROUP + i
                DQ[m * H : (m + 1) * H, h * HD : (h + 1) * HD] = out[i * H : (i + 1) * H]

    class Sums:
        def __init__(self, l):
            self.l = slot(l)
            self.ss, self.sr = take(2), take(2)
            self.xs, self.xr = take(2 * n_ctx), take(2 * n_ctx)

        def swap(self, m):
            send(
                DKV.at[:, :, other, m], SWAP.at[self.l, m], self.ss + m, self.sr + m, partner,
                None, kv_pending,
            )

        def spread(self, m):
            arrive(SWAP.at[self.l, m], self.sr + m)
            for g in range(KV):
                for cc in range(n_ctx):
                    both = DKV[g, cc, s, m].astype(F32) + SWAP[self.l, m, g, cc].astype(F32)
                    DKV[g, cc, s, m] = both.astype(BF)
            for d in range(1, n_ctx):
                peer = lax.rem(c + d, n_ctx)
                send(
                    DKV.at[:, peer, s, m], PILE.at[self.l, c, m], self.xs + m * n_ctx + peer,
                    self.xr + m * n_ctx + c, {"ctx": peer}, None if m == 0 else peer < c,
                    kv_pending,
                )

        def total(self, m):
            for g in range(KV):
                DKO[g, m] = DKV[g, c, s, m].astype(F32)
            for d in range(1, n_ctx):
                peer = lax.rem(c + n_ctx - d, n_ctx)
                there = None if m == 0 else peer > c
                ref = PILE.at[self.l, peer, m]
                arrive(ref, self.xr + m * n_ctx + peer, there)

                def add(peer=peer):
                    for g in range(KV):
                        DKO[g, m] = DKO[g, m] + PILE[self.l, peer, m, g].astype(F32)

                when(there, add)

    class Reduce:
        def __init__(self, part, got, cut):
            self.part, self.got, self.cut, self.out = part, got, cut, got
            self.ps, self.pr = take(), take()
            self.rs, self.rr, self.gs, self.gr = take(n_ctx), take(n_ctx), take(n_ctx), take(n_ctx)

        def give(self, l):
            send(self.part.at[l], self.got, self.ps, self.pr, partner, s != l)

        def scatter(self, l):
            arrive(self.got, self.pr, s == l)

            @pl.when(s == l)
            def _():
                for k in range(n_ctx):
                    both = self.part[l, k].astype(F32) + self.got[k].astype(F32)
                    self.part[l, k] = both.astype(BF)
                self.cut[c] = self.part[l, c]

            for d in range(1, n_ctx):
                peer = lax.rem(c + d, n_ctx)
                send(
                    self.part.at[l, peer], self.cut.at[c], self.rs + peer, self.rr + c,
                    {"ctx": peer}, s == l,
                )

        def gather(self, l):
            for d in range(1, n_ctx):
                peer = lax.rem(c + n_ctx - d, n_ctx)
                arrive(self.cut.at[peer], self.rr + peer, s == l)

            @pl.when(s == l)
            def _():
                total = self.cut[0].astype(F32)
                for cc in range(1, n_ctx):
                    total = total + self.cut[cc].astype(F32)
                self.out[c] = total.astype(BF)

            for d in range(1, n_ctx):
                peer = lax.rem(c + d, n_ctx)
                ref = self.out.at[c]
                send(ref, ref, self.gs + peer, self.gr + c, {"ctx": peer}, s == l)

        def end(self):
            for d in range(1, n_ctx):
                peer = lax.rem(c + n_ctx - d, n_ctx)
                arrive(self.out.at[peer], self.gr + peer)

    red_m = Reduce(PM, RM, CM)
    red_o = Reduce(PO, RO, CO)
    red_a = Reduce(PA, RA, CA)

    def backward(l, e, h, hook):
        ga, gm = GN[l, 0:1], GN[l, 1:2]
        eb = e.astype(BF)
        zz = Z[l]
        dz = jnp.zeros((T, D), F32)
        for k in range(n_wt):
            j = lax.rem(w + k, n_wt)
            da = nn(eb, MW[l, j, 2 * D :])
            if z.keep:
                g, up = G[l, k], UP[l, k]
            else:
                g, up = nn(zz, MW[l, j, :D]), nn(zz, MW[l, j, D : 2 * D])
            sg = jax.nn.sigmoid(g)
            dg = (da * up * sg * (1.0 + g * (1.0 - sg))).astype(BF)
            du = (da * g * sg).astype(BF)
            if k == 0:
                DG[...] = dg
                DU[...] = du
            dz = dz + nt(dg, MW[l, j, :D]) + nt(du, MW[l, j, D : 2 * D])
        n2, r2 = N2[l], R2[l]
        m2 = dz * gm
        dh2 = e + r2 * (m2 - n2 * jnp.mean(m2 * n2, -1, keepdims=True))
        ob = dh2.astype(BF)
        wide = jnp.concatenate([jnp.zeros((T, z.shift), BF), ob], 1) if z.shift else ob
        do = nt(wide, W[l, :, z.tail :]).astype(BF)
        o = O[l]
        prod = do.astype(F32) * o.astype(F32)
        blank = jnp.zeros((T, HD), BF)
        for h_i in range(HEADS):
            t = jnp.concatenate([blank, head(do, h_i)], 1)
            g, at = h_i // GROUP, h_i % GROUP * H
            for m in range(2):
                DO[g, m, at : at + H] = t[m * H : (m + 1) * H]
        for g in range(KV):
            for m in range(2):
                stacked = jnp.concatenate(
                    [head(prod, g * GROUP + i)[m * H : (m + 1) * H] for i in range(GROUP)], 0
                )
                DEL[g, m] = jnp.sum(jnp.transpose(stacked), 0, keepdims=True)

        grads = [tn(zz, DG[...]), tn(zz, DU[...]), tn(eb, ACT[l])]
        grads = jnp.concatenate(grads, 0)
        g_o = tn(column_slice(o), ob)
        tall, thin = 3 * D // n_ctx, D // n_ctx
        for k in range(n_ctx):
            PM[l, k] = grads[k * tall : (k + 1) * tall].astype(BF)
            PO[l, k] = g_o[:, k * thin : (k + 1) * thin].astype(BF)
        GV[l, 1:2] = jnp.sum(dz * n2, 0, keepdims=True)
        hook[0]()
        if l == 0 and not z.keep:
            flush()
            take_turn(1, True)
            u = (h * R1[l] * ga).astype(BF)
            store_kv(l, nn(u, W[l, :, : KV * LANES]))
            sems = gather_kv(l)
            end_kv(l, 0, sems)
            end_kv(l, 1, sems)
        flush(kv_pending)
        DKV[...] = jnp.zeros(DKV.shape, BF)
        low, high = bounds(1)
        split = jnp.maximum(low, n_ctx)
        carry = attend_back(l, 1, (split, high), None)
        sums = Sums(l)
        if l == 0 and not z.keep:
            take_turn(2, True)
        sums.swap(1)
        hook[1]()
        attended_back(1, attend_back(l, 1, (low, split), carry))
        sums.spread(1)
        attended_back(0, attend_back(l, 0, bounds(0), None))
        sums.swap(0)
        hook[2]()
        n1 = h * R1[l]
        u = (n1 * ga).astype(BF)
        sums.spread(0)
        sums.total(1)
        sums.total(0)
        hook[3]()
        parts = [
            rope_back(DKO[g].reshape(T, LANES), kcos, ksa, ksb).astype(BF) for g in range(KV)
        ]
        for i in range(q_tiles):
            at = i * LANES
            t = rope_back(DQ[:, at : at + LANES], cos, sa, sb)
            if at + LANES > QW:
                t = jnp.where(is_key, t, 0.0)
            parts.append(t.astype(BF))
        dqkv = jnp.concatenate(parts, 1)
        g_a = tn(column_slice(u), dqkv)
        thin = z.qkv // n_ctx
        for k in range(n_ctx):
            PA[l, k] = g_a[:, k * thin : (k + 1) * thin].astype(BF)
        red_a.give(l)
        du_in = nt(dqkv, W[l, :, : z.lead])
        m1 = du_in * ga
        e_next = (dh2 + R1[l] * (m1 - n1 * jnp.mean(m1 * n1, -1, keepdims=True))).astype(BF)
        store_rows(YD.at[l], e_next)
        GV[l, 0:1] = jnp.sum(du_in * n1, 0, keepdims=True)
        return e_next

    def nothing():
        pass

    def last_0():
        red_m.give(1)
        red_o.give(1)

    def last_1():
        red_m.scatter(1)
        red_o.scatter(1)

    def last_3():
        red_m.gather(1)
        red_o.gather(1)

    def back_0():
        red_m.give(0)
        red_o.give(0)
        red_a.scatter(1)

    def back_1():
        red_m.scatter(0)
        red_o.scatter(0)
        red_a.gather(1)

    def back_3():
        red_m.gather(0)
        red_o.gather(0)

    e1 = rows_of(E).astype(F32)
    e0 = backward(1, e1, mid.astype(F32), (last_0, last_1, nothing, last_3))
    backward(0, e0.astype(F32), h0, (back_0, back_1, nothing, back_3))
    gp, gq, gx, gy = take(), take(), take(n_ctx), take(n_ctx)
    send(GV.at[other], GT, gp, gq, partner)
    dacts_end = give_rows(YD, dacts_ref)
    red_a.scatter(0)
    arrive(GT, gq)
    GR[c] = GV[s] + GT[...]
    for d in range(1, n_ctx):
        peer = lax.rem(c + d, n_ctx)
        send(GR.at[c], GR.at[c], gx + peer, gy + c, {"ctx": peer})
    red_a.gather(0)
    for d in range(1, n_ctx):
        peer = lax.rem(c + n_ctx - d, n_ctx)
        arrive(GR.at[peer], gy + peer)
    gain = GR[0]
    for cc in range(1, n_ctx):
        gain = gain + GR[cc]
    gain_ref[...] = column_slice(gain)
    red_m.end()
    red_o.end()
    red_a.end()
    acts_end()
    dacts_end()
    flush(kv_pending)
    flush()


def finish(n_ctx, acts, dacts, mlp, out, attn, gain, *outs):
    acts_ref, dacts_ref, ga, gwq, gwk, gwv, gwo, gm, *wide = outs
    acts_ref[0] = acts[...]
    dacts_ref[0] = dacts[...]
    ga[...] = gain[0:1]
    gm[...] = gain[1:2]
    total = jnp.concatenate([attn[k] for k in range(n_ctx)], 1).astype(F32)
    for g in range(KV):
        at = g * LANES
        gwk[0, :, g * HD : (g + 1) * HD] = total[:, at : at + HD]
        gwv[0, :, g * HD : (g + 1) * HD] = total[:, at + HD : at + LANES]
    gwq[0] = total[:, 2 * KVW :]
    gwo[0] = jnp.concatenate([out[k] for k in range(n_ctx)], 1).astype(F32)
    rows = jnp.concatenate([mlp[k].astype(F32) for k in range(n_ctx)], 0)
    size = wide[0].shape[1]
    for i, ref in enumerate(wide):
        ref[0] = rows[i * size : (i + 1) * size]


def local(
    sizes, inputs, doc_start, attn_gain, w_q, w_k, w_v, w_o, mlp_gain, w_gate, w_up, w_down,
    cotangent,
):
    z = Shape(sizes, inputs, w_q, w_gate)
    n_ctx, n_wt, H, T, R = z.n_ctx, z.n_wt, z.half, z.tokens, z.block
    near, D, F, rows = z.near, z.width, z.hidden, z.rows
    freq = np.float32(1.0 / THETA ** (np.arange(HD // 2) * 2.0 / HD))
    freq = jnp.asarray(np.tile(freq, LANES // (HD // 2))[None])
    vm = pl.BlockSpec(memory_space=pltpu.VMEM)
    hbm = pl.BlockSpec(memory_space=pl.ANY)
    shape = jax.ShapeDtypeStruct
    tall, thin, thin_a = 3 * D // n_ctx, D // n_ctx, z.qkv // n_ctx
    sums = [
        shape((2, rows, D), BF), shape((2, rows, D), BF), shape((n_ctx, tall, F), BF),
        shape((n_ctx, z.slice, thin), BF), shape((n_ctx, z.slice, thin_a), BF),
        shape((8, z.slice), F32),
    ]
    outs = [
        shape((1, 2, rows, D), BF), shape((1, 2, rows, D), BF), shape((1, z.slice), F32),
        shape((1, z.slice, QW), F32), shape((1, z.slice, KVW), F32),
        shape((1, z.slice, KVW), F32), shape((1, z.slice, D), F32), shape((1, z.slice), F32),
        shape((1, D, F), F32), shape((1, D, F), F32), shape((1, D, F), F32),
    ]
    layers = 2 if z.keep else 1
    keep = (n_wt, T, F) if z.keep else (1, 8, LANES)
    vmem = pltpu.VMEM
    scratch = [
        vmem((2, n_wt * z.slice, z.cols), BF),
        vmem((2, n_wt, 3 * D, F), BF),
        vmem((near, 2, rows, D), BF),
        vmem((near, 2, rows, D), BF),
        vmem((2, rows, D), BF),
        vmem((2, 8, D), F32),
        vmem((layers, KV, n_ctx, 2, 2, H, LANES), BF),
        vmem((2, KV, 2, GROUP * H, LANES), BF),
        vmem((2, T, QW), BF),
        vmem((2, KV, 2, 1, GROUP * H), F32),
        vmem((2, T, 1), F32),
        vmem((2, T, D), F32),
        vmem((2, T, 1), F32),
        vmem((2, T, D), BF),
        vmem((2,) + keep, F32),
        vmem((2,) + keep, F32),
        vmem((2, T, F), BF),
        vmem((T, F), BF),
        vmem((T, F), BF),
        vmem((KV, 2, GROUP * H, LANES), BF),
        vmem((KV, 2, 1, GROUP * H), F32),
        vmem((T, -(-QW // LANES) * LANES), F32),
        vmem((KV, n_ctx, 2, 2, H, LANES), BF),
        vmem((KV, 2, H, LANES), F32),
        vmem((layers, 2, KV, n_ctx, H, LANES), BF),
        vmem((layers, n_ctx, 2, KV, H, LANES), BF),
        vmem((2, n_ctx, tall, F), BF),
        vmem((2, n_ctx, z.slice, thin), BF),
        vmem((2, n_ctx, z.slice, thin_a), BF),
        vmem((n_ctx, tall, F), BF),
        vmem((n_ctx, z.slice, thin), BF),
        vmem((n_ctx, z.slice, thin_a), BF),
        vmem((2, 8, D), F32),
        vmem((8, D), F32),
        vmem((n_ctx, 8, D), F32),
        vmem((2, near, 2, rows, D), BF),
        vmem((2, near, 2, rows, D), BF),
        vmem((2, 1, GROUP * H), jnp.int32),
        vmem((2, 1, GROUP * H), jnp.int32),
        pltpu.SemaphoreType.DMA((N_SEMS + 56 * n_ctx,)),
        pltpu.SemaphoreType.REGULAR((4,)),
    ]
    done = pl.pallas_call(
        functools.partial(kernel, z),
        out_shape=sums,
        in_specs=[vm] * 10 + [hbm] * 3,
        out_specs=[vm] * len(sums),
        scratch_shapes=scratch,
        compiler_params=pltpu.CompilerParams(
            collective_id=0, has_side_effects=True, vmem_limit_bytes=VMEM_LIMIT
        ),
        name="step",
    )(
        inputs, cotangent, doc_start, freq, attn_gain, mlp_gain, w_q, w_k, w_v, w_o, w_gate, w_up,
        jnp.swapaxes(w_down, 1, 2),
    )
    outs = pl.pallas_call(
        functools.partial(finish, n_ctx),
        out_shape=outs,
        in_specs=[vm] * len(sums),
        out_specs=[vm] * len(outs),
        compiler_params=pltpu.CompilerParams(vmem_limit_bytes=VMEM_LIMIT),
        name="finish",
    )(*done)
    return (*outs[:-1], jnp.swapaxes(outs[-1], 1, 2))


def solution(mesh):
    in_specs = (
        P(None, ("ctx", "wt"), None),
        P(),
        P("section", None),
        P("section", "wt", None),
        P("section", "wt", None),
        P("section", "wt", None),
        P("section", "wt", None),
        P("section", None),
        P("section", None, "wt"),
        P("section", None, "wt"),
        P("section", "wt", None),
        P(None, ("ctx", "wt"), None),
    )
    out_specs = (
        P("section", None, ("ctx", "wt"), None),
        P("section", None, ("ctx", "wt"), None),
        P("section", "wt"),
        P("section", "wt", None),
        P("section", "wt", None),
        P("section", "wt", None),
        P("section", "wt", None),
        P("section", "wt"),
        P("section", None, "wt"),
        P("section", None, "wt"),
        P("section", "wt", None),
    )
    sizes = dict(mesh.shape)
    return jax.shard_map(
        functools.partial(local, sizes), mesh=mesh, in_specs=in_specs, out_specs=out_specs,
        check_vma=False,
    )
```

```python
import functools

import jax
import jax.numpy as jnp
import numpy as np
from jax import lax
from jax.experimental import pallas as pl
from jax.experimental.pallas import tpu as pltpu
from jax.sharding import PartitionSpec as P

HEADS = 9
KV = 3
GROUP = HEADS // KV
HD = 64
KVW = KV * HD
QW = HEADS * HD
EPS = 1e-05
THETA = 100000.0
FLOOR = -1e30
BF = jnp.bfloat16
F32 = jnp.float32
VMEM_LIMIT = 62 * 1024 * 1024
MESH = pl.DeviceIdType.MESH
LANES = 128
N_SEMS = 280


def nt(a, b):
    return lax.dot_general(a, b, (((1,), (1,)), ((), ())), preferred_element_type=F32)


def tn(a, b):
    return lax.dot_general(a, b, (((0,), (0,)), ((), ())), preferred_element_type=F32)


def nn(a, b):
    return jnp.dot(a, b, preferred_element_type=F32)


def rope(t, cos, sa, sb):
    return t * cos + pltpu.roll(t, LANES - HD // 2, 1) * sa + pltpu.roll(t, HD // 2, 1) * sb


def rope_back(t, cos, sa, sb):
    return t * cos - pltpu.roll(t, LANES - HD // 2, 1) * sa - pltpu.roll(t, HD // 2, 1) * sb


class Shape:
    def __init__(self, sizes, inputs, w_q, w_gate):
        self.n_ctx, self.n_wt = sizes["ctx"], sizes["wt"]
        self.rows, self.width = inputs.shape[1], inputs.shape[2]
        self.near = self.n_wt // 2
        self.half = self.rows * self.near
        self.tokens = 2 * self.half
        self.block = 2 * self.half
        self.keys = 2 * self.n_ctx * self.block
        self.slice = w_q.shape[1]
        self.hidden = w_gate.shape[2]
        self.qkv = 2 * KVW + QW
        self.cols = self.qkv + self.width
        self.lead = -(-self.qkv // LANES) * LANES
        self.tail = self.qkv // LANES * LANES
        self.shift = self.qkv - self.tail
        self.last_start = self.keys - self.keys // 8 - 1
        self.keep = self.keys <= 4096


def kernel(z, *refs):
    (
        x_ref, cot_ref, start_ref, freq_ref, ga_ref, gm_ref, wq_ref, wk_ref, wv_ref, wo_ref,
        gate_ref, up_ref, down_ref,
    ) = refs[:13]
    acts_ref, dacts_ref, RM, RO, RA, gain_ref = refs[13:19]
    (
        W, MW, X, E, EB, GN, KVB, Q, O, LSE, R1, N2, R2, Z, G, UP, ACT, DG, DU, DO, DEL, DQ,
        DKV, DKO, SWAP, PILE, PM, PO, PA, CM, CO, CA, GV, GT, GR, YA, YD, POS, DOC, sem, turn,
    ) = refs[19:]
    n_ctx, n_wt, H, T, R = z.n_ctx, z.n_wt, z.half, z.tokens, z.block
    near = z.near
    s, c, w = lax.axis_index("section"), lax.axis_index("ctx"), lax.axis_index("wt")
    other = 1 - s
    partner = {"section": other}
    has_left, has_right = w > 0, w < n_wt - 1
    side, seat = lax.div(w, near), lax.rem(w, near)

    used = [0]
    pending = []

    def take(n=1):
        first = used[0]
        used[0] += n
        assert used[0] <= N_SEMS + 56 * n_ctx
        return first

    def when(cond, f):
        if cond is None:
            f()
        else:
            pl.when(cond)(lambda: (f(), None)[1])

    def remote(src, dst, si, ri, where):
        return pltpu.make_async_remote_copy(
            src_ref=src, dst_ref=dst, send_sem=sem.at[si], recv_sem=sem.at[ri],
            device_id=where, device_id_type=MESH,
        )

    def send(src, dst, si, ri, where, cond=None, out=pending):
        copy = remote(src, dst, si, ri, where)
        when(cond, copy.start)
        out.append((cond, copy.wait_send))

    def arrive(dst, ri, cond=None):
        when(cond, remote(dst, dst, ri, ri, partner).wait_recv)

    def post(src, dst, si, ri, where, cond=None, out=pending):
        copy = remote(src, dst, si, ri, where)
        out.append((cond, copy.wait_send))
        return copy.start

    def expect(dst, ri):
        return remote(dst, dst, ri, ri, partner).wait_recv

    def group(cond, *steps):
        def run():
            for step in steps:
                step()

        when(cond, run)

    def flush(out=pending):
        sets = {}
        for cond, wait in out:
            sets.setdefault(id(cond), (cond, []))[1].append(wait)
        for cond, waits in sets.values():
            group(cond, *waits)
        out.clear()

    ahead = [lax.rem(c + d, n_ctx) for d in range(n_ctx)]
    behind = [lax.rem(c + n_ctx - d, n_ctx) for d in range(n_ctx)]
    above, below = [p > c for p in ahead], [p < c for p in behind]
    on = (s == 0, s == 1)
    to_right, to_left = [o & has_right for o in on], [o & has_left for o in on]

    barrier = pltpu.get_barrier_semaphore()

    def greet(where):
        pl.semaphore_signal(barrier, inc=1, device_id=where, device_id_type=MESH)

    greet(partner)
    for d in range(1, n_wt):
        greet({"wt": lax.rem(w + d, n_wt)})
    for d in range(1, n_ctx):
        greet({"ctx": lax.rem(c + d, n_ctx)})

    D = z.width
    load = [
        pltpu.make_async_copy(ref.at[0], MW.at[s, w, pl.ds(i * D, D)], sem.at[take()])
        for i, ref in enumerate((gate_ref, up_ref, down_ref))
    ]
    for copy in load:
        copy.start()
    first = pl.multiple_of(w * z.slice, 16)
    wk, wv = wk_ref[0], wv_ref[0]
    pieces = []
    for g in range(KV):
        pieces += [wk[:, g * HD : (g + 1) * HD], wv[:, g * HD : (g + 1) * HD]]
    W[s, pl.ds(first, z.slice), :] = jnp.concatenate(pieces + [wq_ref[0], wo_ref[0]], 1)
    GN[s, 0:1] = ga_ref[...]
    GN[s, 1:2] = gm_ref[...]
    pl.semaphore_wait(barrier, 1 + (n_wt - 1) + (n_ctx - 1))

    gain_send, gain_recv = take(), take()
    send(GN.at[s], GN.at[s], gain_send, gain_recv, partner)

    def rows_start(source, dest):
        sends, recvs = take(n_wt), take(n_wt)
        for d in range(1, n_wt):
            peer = lax.rem(w + d, n_wt)
            send(source, dest.at[seat], sends + peer, recvs + w, {"wt": peer}, side == s)
        return recvs

    def rows_end(dest, recvs):
        for i in range(near):
            k = s * near + i
            arrive(dest.at[i], recvs + k, k != w)

    half_ctx = n_ctx // 2
    bit_a, bit_b = lax.rem(c, 2), lax.rem(lax.div(c, half_ctx), 2)
    peer_a = {"ctx": c + 1 - 2 * bit_a}
    peer_b = {"ctx": c + half_ctx - 2 * half_ctx * bit_b}
    mine_q = (bit_a, 2 + bit_b)
    their_q = (1 - bit_a, 3 - bit_b)

    class Gather:
        def __init__(self, part, whole):
            self.part, self.whole = part, whole
            self.zr, self.right, self.left = take(2 * n_wt), take(2 * n_wt), take(2 * n_wt)
            self.xs, self.xr = take(2 * n_wt), take(2 * n_wt)
            self.ps, self.pr = take(n_wt), take(n_wt)

        def along(self, j, go_right, cond):
            base = self.right if go_right else self.left
            where = {"wt": lax.rem(w + 1 if go_right else w + n_wt - 1, n_wt)}
            out = []
            for i in range(2):
                ref = self.part(s, j, mine_q[i])
                out.append(post(ref, ref, base + 2 * j + i, self.zr + 2 * j + i, where, cond))
            return out

        def over(self, j, cond):
            ref = self.whole(s, j)
            return post(ref, ref, self.ps + j, self.pr + j, partner, cond)

        def start(self, l):
            group(to_right[l], *self.along(w, True, to_right[l]))
            group(to_left[l], *self.along(w, False, to_left[l]))
            group(on[l], self.over(w, on[l]))

        def from_side(self, l, t):
            low, high = w - t, w + t
            return (
                (lax.rem(low + n_wt, n_wt), on[l] & (low >= 0), True, has_right),
                (lax.rem(high, n_wt), on[l] & (high < n_wt), False, has_left),
            )

        def hop(self, l, t):
            for j, there, go_right, more in self.from_side(l, t):
                steps = []
                for i in range(2):
                    steps.append(expect(self.part(s, j, mine_q[i]), self.zr + 2 * j + i))
                if t < n_wt - 1:
                    further = self.along(j, go_right, there & more)
                    steps.append(functools.partial(group, more, *further))
                for i, peer in enumerate((peer_a, peer_b)):
                    ref = self.part(s, j, mine_q[i])
                    steps.append(
                        post(ref, ref, self.xs + 2 * j + i, self.xr + 2 * j + i, peer, there)
                    )
                group(there, *steps)

        def cross(self, l, t):
            for j, there, go_right, more in self.from_side(l, t):
                steps = []
                for i in range(2):
                    steps.append(expect(self.part(s, j, their_q[i]), self.xr + 2 * j + i))
                group(there, *steps, self.over(j, there))

        def end(self, l):
            group(on[1 - l], *[expect(self.whole(other, j), self.pr + j) for j in range(n_wt)])

    quarter = z.cols // 4
    g_w = Gather(
        lambda l, j, q: W.at[
            l, pl.ds(pl.multiple_of(j * z.slice, 16), z.slice),
            pl.ds(pl.multiple_of(q * quarter, LANES), quarter),
        ],
        lambda l, j: W.at[l, pl.ds(pl.multiple_of(j * z.slice, 16), z.slice)],
    )
    quarter_m = 3 * D // 4
    g_m = Gather(
        lambda l, j, q: MW.at[l, j, pl.ds(pl.multiple_of(q * quarter_m, 16), quarter_m)],
        lambda l, j: MW.at[l, j],
    )

    x_recv = rows_start(x_ref, X)
    g_w.start(0)
    own_x = pltpu.make_async_copy(x_ref, X.at[seat], sem.at[take()])
    when(side == s, own_x.start)

    lane = lax.broadcasted_iota(jnp.int32, (T, LANES), 1)
    is_key = lane < HD
    angles = []
    for m in range(2):
        at = c * R + s * H
        doc = start_ref[m : m + 1, pl.ds(pl.multiple_of(at, LANES), H)]
        pos = m * n_ctx * R + at + lax.broadcasted_iota(jnp.int32, (1, H), 1)
        POS[m] = jnp.concatenate([pos] * GROUP, 1)
        DOC[m] = jnp.concatenate([doc] * GROUP, 1)
        gap = jnp.broadcast_to((pos - doc).astype(F32), (LANES, H))
        angles.append(jnp.transpose(gap) * freq_ref[...])
    angles = jnp.concatenate(angles, 0)
    cos, sin = jnp.cos(angles), jnp.sin(angles)
    first_half = lax.rem(lane, HD) < HD // 2
    sa, sb = jnp.where(first_half, -sin, 0.0), jnp.where(first_half, 0.0, sin)
    kcos = jnp.where(is_key, cos, 1.0)
    ksa, ksb = jnp.where(is_key, sa, 0.0), jnp.where(is_key, sb, 0.0)
    EB[...] = cot_ref[...].astype(BF)

    for copy in load:
        copy.wait()
    for t in range(1, n_wt):
        g_w.hop(0, t)
        if t == 1:
            g_m.start(0)
    for t in range(1, n_wt):
        g_w.cross(0, t)
    rows_end(X, x_recv)
    when(side == s, own_x.wait)
    arrive(GN.at[other], gain_recv)
    g_w.end(0)

    def rows_of(ref):
        return jnp.concatenate([ref[i, m] for m in range(2) for i in range(near)], 0)

    def store_rows(ref, value):
        for m in range(2):
            for i in range(near):
                at = m * H + i * z.rows
                ref[i, m] = value[at : at + z.rows]

    def head(value, h):
        return value[:, h * HD : (h + 1) * HD]

    q_tiles = -(-QW // LANES)

    def bounds(m):
        high = m * n_ctx + c
        start = high * R + s * H
        low = jnp.where(start >= z.last_start, z.last_start // R, 0)
        return low, high + 1

    def place_of(kb):
        return lax.rem(kb, n_ctx), lax.div(kb, n_ctx)

    def allowed(kb, m):
        at = kb * R + lax.broadcasted_iota(jnp.int32, (R, GROUP * H), 0)
        return (at <= POS[m]) & (at >= DOC[m])

    def slot(l):
        return l if z.keep else 0

    def take_turn(i, near_too):
        for d in range(1, n_ctx):
            pl.semaphore_signal(
                turn.at[i], inc=1, device_id={"ctx": lax.rem(c + d, n_ctx)}, device_id_type=MESH
            )
        if near_too:
            pl.semaphore_signal(turn.at[i], inc=1, device_id=partner, device_id_type=MESH)
        pl.semaphore_wait(turn.at[i], n_ctx - 1 + int(near_too))

    def keys_of(l, g, cc, mm):
        return KVB[slot(l), g, cc, :, mm].reshape(R, LANES)

    def gather_kv(l):
        out = []
        for m in range(2):
            ks, kr, fs, fr = take(n_ctx + 1), take(n_ctx), take(n_ctx), take(n_ctx)
            ref = KVB.at[slot(l), :, c, s, m]
            send(ref, ref, ks + n_ctx, fr + c, partner)
            for d in range(1, n_ctx):
                peer = ahead[d]
                send(ref, ref, ks + peer, kr + c, {"ctx": peer}, None if m == 0 else above[d])
            out.append((kr, fs, fr))
        return out

    def end_kv(l, m, sems):
        kr, fs, fr = sems[m]
        for d in range(1, n_ctx):
            peer, there = behind[d], None if m == 0 else below[d]
            ref = KVB.at[slot(l), :, peer, s, m]
            group(
                there, expect(ref, kr + peer),
                post(ref, ref, fs + peer, fr + peer, partner, there),
            )
        arrive(KVB.at[slot(l), :, c, other, m], fr + c)
        for d in range(1, n_ctx):
            peer, there = behind[d], None if m == 0 else below[d]
            arrive(KVB.at[slot(l), :, peer, other, m], fr + peer, there)

    def store_kv(l, kvq):
        for g in range(KV):
            t = rope(kvq[:, g * LANES : (g + 1) * LANES], kcos, ksa, ksb).astype(BF)
            for m in range(2):
                KVB[slot(l), g, c, s, m] = t[m * H : (m + 1) * H]

    def attend(l, m, loop, carry):
        def step(kb, carry):
            cc, mm = place_of(kb)
            ok = allowed(kb, m)
            out = []
            for g in range(KV):
                top, total, acc = carry[3 * g : 3 * g + 3]
                kv = keys_of(l, g, cc, mm)
                sc = jnp.where(ok, nt(kv, Q[l, g, m]), FLOOR)
                new = jnp.maximum(top, jnp.max(sc, 0, keepdims=True))
                scale = jnp.exp(top - new)
                p = jnp.exp(sc - new)
                total = total * scale + jnp.sum(p, 0, keepdims=True)
                acc = acc * scale + tn(kv, p.astype(BF))
                out += [new, total, acc]
            return tuple(out)

        if carry is None:
            carry = (
                jnp.full((1, GROUP * H), FLOOR, F32),
                jnp.zeros((1, GROUP * H), F32),
                jnp.zeros((LANES, GROUP * H), F32),
            ) * KV
        return lax.fori_loop(*loop, step, carry)

    def attended(l, m, carry):
        for g in range(KV):
            top, total, acc = carry[3 * g : 3 * g + 3]
            out = jnp.transpose(acc[HD:] / total).astype(BF)
            for i in range(GROUP):
                h = g * GROUP + i
                O[l, m * H : (m + 1) * H, h * HD : (h + 1) * HD] = out[i * H : (i + 1) * H]
            LSE[l, g, m] = top + jnp.log(total)

    def forward(l, h, hook):
        ga, gm = GN[l, 0:1], GN[l, 1:2]
        r1 = lax.rsqrt(jnp.mean(h * h, -1, keepdims=True) + EPS)
        R1[l] = r1
        u = (h * r1 * ga).astype(BF)
        kvq = nn(u, W[l, :, : z.lead])
        if l == 1 and not z.keep:
            flush()
            take_turn(0, True)
        store_kv(l, kvq)
        sems = gather_kv(l)
        hook[4]()
        for i in range(q_tiles):
            at = KV * LANES + i * LANES
            t = rope(kvq[:, at : at + LANES], cos, sa, sb) * 0.125
            for k in range(LANES // HD):
                hd = i * (LANES // HD) + k
                if hd < HEADS:
                    moved = pltpu.roll(t, HD, 1) if k else t
                    moved = jnp.where(is_key, moved, 0.0).astype(BF)
                    g, at_h = hd // GROUP, hd % GROUP * H
                    for m in range(2):
                        Q[l, g, m, at_h : at_h + H] = moved[m * H : (m + 1) * H]
        end_kv(l, 0, sems)
        hook[0]()
        attended(l, 0, attend(l, 0, bounds(0), None))
        low, high = bounds(1)
        split = jnp.maximum(low, n_ctx)
        carry = attend(l, 1, (low, split), None)
        end_kv(l, 1, sems)
        hook[1]()
        attended(l, 1, attend(l, 1, (split, high), carry))
        hook[2]()
        h2 = h + nn(O[l], W[l, :, z.tail :])[:, z.shift :]
        r2 = lax.rsqrt(jnp.mean(h2 * h2, -1, keepdims=True) + EPS)
        n2 = h2 * r2
        zz = (n2 * gm).astype(BF)
        R2[l] = r2
        N2[l] = n2
        Z[l] = zz
        hook[3]()
        total = h2
        for k in range(n_wt):
            j = lax.rem(w + k, n_wt)
            g = nn(zz, MW[l, j, :D])
            up = nn(zz, MW[l, j, D : 2 * D])
            act = (g * jax.nn.sigmoid(g) * up).astype(BF)
            if k == 0:
                ACT[l] = act
            if z.keep:
                G[l, k] = g
                UP[l, k] = up
            total = total + nt(act, MW[l, j, 2 * D :])
        out = total.astype(BF)
        store_rows(YA.at[l], out)
        return out

    def first_a():
        g_m.hop(0, 1)

    def first_0():
        g_m.hop(0, 2)
        g_m.cross(0, 1)
        g_w.start(1)

    def first_1():
        g_m.hop(0, 3)
        g_m.cross(0, 2)
        g_w.hop(1, 1)

    def first_2():
        g_m.cross(0, 3)
        g_w.hop(1, 2)
        g_w.cross(1, 1)
        g_m.start(1)

    def first_3():
        g_w.hop(1, 3)
        g_w.cross(1, 2)
        g_m.end(0)

    def second_a():
        g_m.hop(1, 1)

    def second_0():
        g_m.hop(1, 2)
        g_m.cross(1, 1)

    def second_1():
        g_m.hop(1, 3)
        g_m.cross(1, 2)

    def second_2():
        g_m.cross(1, 3)
        flush(early)

    def second_3():
        g_m.end(1)

    early = []
    h0 = rows_of(X).astype(F32)
    mid = forward(0, h0, (first_0, first_1, first_2, first_3, first_a))
    g_w.cross(1, 3)
    early.extend(pending)
    pending.clear()
    e_recv = rows_start(EB, E)
    own_e = pltpu.make_async_copy(EB, E.at[seat], sem.at[take()])
    when(side == s, own_e.start)
    g_w.end(1)
    forward(1, mid.astype(F32), (second_0, second_1, second_2, second_3, second_a))

    rows_end(E, e_recv)
    when(side == s, own_e.wait)

    def give_rows(ref, out_ref):
        si, ri, li = take(), take(), take()
        send(ref.at[other, seat], out_ref, si, ri, partner, side == s)
        copy = pltpu.make_async_copy(ref.at[s, seat], out_ref, sem.at[li])
        when(side == s, copy.start)

        def end():
            when(side == s, copy.wait)
            arrive(out_ref, ri, side != s)

        return end

    acts_end = give_rows(YA, acts_ref)

    def column_slice(value):
        out = value[:, : z.slice]
        for j in range(1, n_wt):
            out = jnp.where(w == j, value[:, j * z.slice : (j + 1) * z.slice], out)
        return out

    kv_pending = []

    def attend_back(l, m, loop, carry):
        def step(kb, carry):
            cc, mm = place_of(kb)
            ok = allowed(kb, m)
            out = []
            for g in range(KV):
                dq = carry[g]
                kv = keys_of(l, g, cc, mm)
                q, do = Q[l, g, m], DO[g, m]
                sc = jnp.where(ok, nt(kv, q), FLOOR)
                p = jnp.exp(sc - LSE[l, g, m])
                ds = (p * (nt(kv, do) - DEL[g, m])).astype(BF)
                tile = nn(ds, q) + nn(p.astype(BF), do)
                old = DKV[g, cc, :, mm].reshape(R, LANES).astype(F32)
                DKV[g, cc, :, mm] = (old + tile).astype(BF).reshape(2, H, LANES)
                out.append(dq + tn(kv, ds))
            return tuple(out)

        if carry is None:
            carry = (jnp.zeros((LANES, GROUP * H), F32),) * KV
        return lax.fori_loop(*loop, step, carry)

    def attended_back(m, carry):
        for g in range(KV):
            out = jnp.transpose(carry[g][:HD] * 0.125)
            for i in range(GROUP):
                h = g * GROUP + i
                DQ[m * H : (m + 1) * H, h * HD : (h + 1) * HD] = out[i * H : (i + 1) * H]

    class Sums:
        def __init__(self, l):
            self.l = slot(l)
            self.ss, self.sr = take(2), take(2)
            self.xs, self.xr = take(2 * n_ctx), take(2 * n_ctx)

        def swap(self, m):
            send(
                DKV.at[:, :, other, m], SWAP.at[self.l, m], self.ss + m, self.sr + m, partner,
                None, kv_pending,
            )

        def spread(self, m):
            arrive(SWAP.at[self.l, m], self.sr + m)
            for g in range(KV):
                for cc in range(n_ctx):
                    both = DKV[g, cc, s, m].astype(F32) + SWAP[self.l, m, g, cc].astype(F32)
                    DKV[g, cc, s, m] = both.astype(BF)
            for d in range(1, n_ctx):
                peer = lax.rem(c + d, n_ctx)
                send(
                    DKV.at[:, peer, s, m], PILE.at[self.l, c, m], self.xs + m * n_ctx + peer,
                    self.xr + m * n_ctx + c, {"ctx": peer}, None if m == 0 else peer < c,
                    kv_pending,
                )

        def total(self, m):
            for g in range(KV):
                DKO[g, m] = DKV[g, c, s, m].astype(F32)
            for d in range(1, n_ctx):
                peer = lax.rem(c + n_ctx - d, n_ctx)
                there = None if m == 0 else peer > c
                ref = PILE.at[self.l, peer, m]
                arrive(ref, self.xr + m * n_ctx + peer, there)

                def add(peer=peer):
                    for g in range(KV):
                        DKO[g, m] = DKO[g, m] + PILE[self.l, peer, m, g].astype(F32)

                when(there, add)

    class Reduce:
        def __init__(self, part, got, cut):
            self.part, self.got, self.cut, self.out = part, got, cut, got
            self.ps, self.pr = take(), take()
            self.rs, self.rr, self.gs, self.gr = take(n_ctx), take(n_ctx), take(n_ctx), take(n_ctx)

        def give(self, l):
            send(self.part.at[l], self.got, self.ps, self.pr, partner, on[1 - l])

        def scatter(self, l):
            def add():
                for k in range(n_ctx):
                    both = self.part[l, k].astype(F32) + self.got[k].astype(F32)
                    self.part[l, k] = both.astype(BF)
                self.cut[c] = self.part[l, c]

            steps = [expect(self.got, self.pr), add]
            for d in range(1, n_ctx):
                peer = ahead[d]
                steps.append(
                    post(
                        self.part.at[l, peer], self.cut.at[c], self.rs + peer, self.rr + c,
                        {"ctx": peer}, on[l],
                    )
                )
            group(on[l], *steps)

        def gather(self, l):
            def add():
                total = self.cut[0].astype(F32)
                for cc in range(1, n_ctx):
                    total = total + self.cut[cc].astype(F32)
                self.out[c] = total.astype(BF)

            steps = [expect(self.cut.at[p], self.rr + p) for p in behind[1:]] + [add]
            for peer in ahead[1:]:
                ref = self.out.at[c]
                steps.append(
                    post(ref, ref, self.gs + peer, self.gr + c, {"ctx": peer}, on[l])
                )
            group(on[l], *steps)

        def end(self):
            for d in range(1, n_ctx):
                peer = lax.rem(c + n_ctx - d, n_ctx)
                arrive(self.out.at[peer], self.gr + peer)

    red_m = Reduce(PM, RM, CM)
    red_o = Reduce(PO, RO, CO)
    red_a = Reduce(PA, RA, CA)

    def backward(l, e, h, hook):
        ga, gm = GN[l, 0:1], GN[l, 1:2]
        eb = e.astype(BF)
        zz = Z[l]
        dz = jnp.zeros((T, D), F32)
        for k in range(n_wt):
            j = lax.rem(w + k, n_wt)
            da = nn(eb, MW[l, j, 2 * D :])
            if z.keep:
                g, up = G[l, k], UP[l, k]
            else:
                g, up = nn(zz, MW[l, j, :D]), nn(zz, MW[l, j, D : 2 * D])
            sg = jax.nn.sigmoid(g)
            dg = (da * up * sg * (1.0 + g * (1.0 - sg))).astype(BF)
            du = (da * g * sg).astype(BF)
            if k == 0:
                DG[...] = dg
                DU[...] = du
            dz = dz + nt(dg, MW[l, j, :D]) + nt(du, MW[l, j, D : 2 * D])
        n2, r2 = N2[l], R2[l]
        m2 = dz * gm
        dh2 = e + r2 * (m2 - n2 * jnp.mean(m2 * n2, -1, keepdims=True))
        ob = dh2.astype(BF)
        wide = jnp.concatenate([jnp.zeros((T, z.shift), BF), ob], 1) if z.shift else ob
        do = nt(wide, W[l, :, z.tail :]).astype(BF)
        o = O[l]
        prod = do.astype(F32) * o.astype(F32)
        blank = jnp.zeros((T, HD), BF)
        for h_i in range(HEADS):
            t = jnp.concatenate([blank, head(do, h_i)], 1)
            g, at = h_i // GROUP, h_i % GROUP * H
            for m in range(2):
                DO[g, m, at : at + H] = t[m * H : (m + 1) * H]
        for g in range(KV):
            for m in range(2):
                stacked = jnp.concatenate(
                    [head(prod, g * GROUP + i)[m * H : (m + 1) * H] for i in range(GROUP)], 0
                )
                DEL[g, m] = jnp.sum(jnp.transpose(stacked), 0, keepdims=True)

        grads = [tn(zz, DG[...]), tn(zz, DU[...]), tn(eb, ACT[l])]
        grads = jnp.concatenate(grads, 0)
        g_o = tn(column_slice(o), ob)
        tall, thin = 3 * D // n_ctx, D // n_ctx
        for k in range(n_ctx):
            PM[l, k] = grads[k * tall : (k + 1) * tall].astype(BF)
            PO[l, k] = g_o[:, k * thin : (k + 1) * thin].astype(BF)
        GV[l, 1:2] = jnp.sum(dz * n2, 0, keepdims=True)
        hook[0]()
        if l == 0 and not z.keep:
            flush()
            take_turn(1, True)
            u = (h * R1[l] * ga).astype(BF)
            store_kv(l, nn(u, W[l, :, : KV * LANES]))
            sems = gather_kv(l)
            end_kv(l, 0, sems)
            end_kv(l, 1, sems)
        flush(kv_pending)
        DKV[...] = jnp.zeros(DKV.shape, BF)
        low, high = bounds(1)
        split = jnp.maximum(low, n_ctx)
        carry = attend_back(l, 1, (split, high), None)
        sums = Sums(l)
        if l == 0 and not z.keep:
            take_turn(2, True)
        sums.swap(1)
        hook[1]()
        attended_back(1, attend_back(l, 1, (low, split), carry))
        sums.spread(1)
        attended_back(0, attend_back(l, 0, bounds(0), None))
        sums.swap(0)
        hook[2]()
        n1 = h * R1[l]
        u = (n1 * ga).astype(BF)
        sums.spread(0)
        sums.total(1)
        sums.total(0)
        hook[3]()
        parts = [
            rope_back(DKO[g].reshape(T, LANES), kcos, ksa, ksb).astype(BF) for g in range(KV)
        ]
        for i in range(q_tiles):
            at = i * LANES
            t = rope_back(DQ[:, at : at + LANES], cos, sa, sb)
            if at + LANES > QW:
                t = jnp.where(is_key, t, 0.0)
            parts.append(t.astype(BF))
        dqkv = jnp.concatenate(parts, 1)
        g_a = tn(column_slice(u), dqkv)
        thin = z.qkv // n_ctx
        for k in range(n_ctx):
            PA[l, k] = g_a[:, k * thin : (k + 1) * thin].astype(BF)
        red_a.give(l)
        du_in = nt(dqkv, W[l, :, : z.lead])
        m1 = du_in * ga
        e_next = (dh2 + R1[l] * (m1 - n1 * jnp.mean(m1 * n1, -1, keepdims=True))).astype(BF)
        store_rows(YD.at[l], e_next)
        GV[l, 0:1] = jnp.sum(du_in * n1, 0, keepdims=True)
        return e_next

    def nothing():
        pass

    def last_0():
        red_m.give(1)
        red_o.give(1)

    def last_1():
        red_m.scatter(1)
        red_o.scatter(1)

    def last_3():
        red_m.gather(1)
        red_o.gather(1)

    def back_0():
        red_m.give(0)
        red_o.give(0)
        red_a.scatter(1)

    def back_1():
        red_m.scatter(0)
        red_o.scatter(0)
        red_a.gather(1)

    def back_3():
        red_m.gather(0)
        red_o.gather(0)

    e1 = rows_of(E).astype(F32)
    e0 = backward(1, e1, mid.astype(F32), (last_0, last_1, nothing, last_3))
    backward(0, e0.astype(F32), h0, (back_0, back_1, nothing, back_3))
    gp, gq, gx, gy = take(), take(), take(n_ctx), take(n_ctx)
    send(GV.at[other], GT, gp, gq, partner)
    dacts_end = give_rows(YD, dacts_ref)
    red_a.scatter(0)
    arrive(GT, gq)
    GR[c] = GV[s] + GT[...]
    for d in range(1, n_ctx):
        peer = lax.rem(c + d, n_ctx)
        send(GR.at[c], GR.at[c], gx + peer, gy + c, {"ctx": peer})
    red_a.gather(0)
    for d in range(1, n_ctx):
        peer = lax.rem(c + n_ctx - d, n_ctx)
        arrive(GR.at[peer], gy + peer)
    gain = GR[0]
    for cc in range(1, n_ctx):
        gain = gain + GR[cc]
    gain_ref[...] = column_slice(gain)
    red_m.end()
    red_o.end()
    red_a.end()
    acts_end()
    dacts_end()
    flush(kv_pending)
    flush()


def finish(n_ctx, acts, dacts, mlp, out, attn, gain, *outs):
    acts_ref, dacts_ref, ga, gwq, gwk, gwv, gwo, gm, *wide = outs
    acts_ref[0] = acts[...]
    dacts_ref[0] = dacts[...]
    ga[...] = gain[0:1]
    gm[...] = gain[1:2]
    total = jnp.concatenate([attn[k] for k in range(n_ctx)], 1).astype(F32)
    for g in range(KV):
        at = g * LANES
        gwk[0, :, g * HD : (g + 1) * HD] = total[:, at : at + HD]
        gwv[0, :, g * HD : (g + 1) * HD] = total[:, at + HD : at + LANES]
    gwq[0] = total[:, 2 * KVW :]
    gwo[0] = jnp.concatenate([out[k] for k in range(n_ctx)], 1).astype(F32)
    rows = jnp.concatenate([mlp[k].astype(F32) for k in range(n_ctx)], 0)
    size = wide[0].shape[1]
    for i, ref in enumerate(wide):
        ref[0] = rows[i * size : (i + 1) * size]


def local(
    sizes, inputs, doc_start, attn_gain, w_q, w_k, w_v, w_o, mlp_gain, w_gate, w_up, w_down,
    cotangent,
):
    z = Shape(sizes, inputs, w_q, w_gate)
    n_ctx, n_wt, H, T, R = z.n_ctx, z.n_wt, z.half, z.tokens, z.block
    near, D, F, rows = z.near, z.width, z.hidden, z.rows
    freq = np.float32(1.0 / THETA ** (np.arange(HD // 2) * 2.0 / HD))
    freq = jnp.asarray(np.tile(freq, LANES // (HD // 2))[None])
    vm = pl.BlockSpec(memory_space=pltpu.VMEM)
    hbm = pl.BlockSpec(memory_space=pl.ANY)
    shape = jax.ShapeDtypeStruct
    tall, thin, thin_a = 3 * D // n_ctx, D // n_ctx, z.qkv // n_ctx
    sums = [
        shape((2, rows, D), BF), shape((2, rows, D), BF), shape((n_ctx, tall, F), BF),
        shape((n_ctx, z.slice, thin), BF), shape((n_ctx, z.slice, thin_a), BF),
        shape((8, z.slice), F32),
    ]
    outs = [
        shape((1, 2, rows, D), BF), shape((1, 2, rows, D), BF), shape((1, z.slice), F32),
        shape((1, z.slice, QW), F32), shape((1, z.slice, KVW), F32),
        shape((1, z.slice, KVW), F32), shape((1, z.slice, D), F32), shape((1, z.slice), F32),
        shape((1, D, F), F32), shape((1, D, F), F32), shape((1, D, F), F32),
    ]
    layers = 2 if z.keep else 1
    keep = (n_wt, T, F) if z.keep else (1, 8, LANES)
    vmem = pltpu.VMEM
    scratch = [
        vmem((2, n_wt * z.slice, z.cols), BF),
        vmem((2, n_wt, 3 * D, F), BF),
        vmem((near, 2, rows, D), BF),
        vmem((near, 2, rows, D), BF),
        vmem((2, rows, D), BF),
        vmem((2, 8, D), F32),
        vmem((layers, KV, n_ctx, 2, 2, H, LANES), BF),
        vmem((2, KV, 2, GROUP * H, LANES), BF),
        vmem((2, T, QW), BF),
        vmem((2, KV, 2, 1, GROUP * H), F32),
        vmem((2, T, 1), F32),
        vmem((2, T, D), F32),
        vmem((2, T, 1), F32),
        vmem((2, T, D), BF),
        vmem((2,) + keep, F32),
        vmem((2,) + keep, F32),
        vmem((2, T, F), BF),
        vmem((T, F), BF),
        vmem((T, F), BF),
        vmem((KV, 2, GROUP * H, LANES), BF),
        vmem((KV, 2, 1, GROUP * H), F32),
        vmem((T, -(-QW // LANES) * LANES), F32),
        vmem((KV, n_ctx, 2, 2, H, LANES), BF),
        vmem((KV, 2, H, LANES), F32),
        vmem((layers, 2, KV, n_ctx, H, LANES), BF),
        vmem((layers, n_ctx, 2, KV, H, LANES), BF),
        vmem((2, n_ctx, tall, F), BF),
        vmem((2, n_ctx, z.slice, thin), BF),
        vmem((2, n_ctx, z.slice, thin_a), BF),
        vmem((n_ctx, tall, F), BF),
        vmem((n_ctx, z.slice, thin), BF),
        vmem((n_ctx, z.slice, thin_a), BF),
        vmem((2, 8, D), F32),
        vmem((8, D), F32),
        vmem((n_ctx, 8, D), F32),
        vmem((2, near, 2, rows, D), BF),
        vmem((2, near, 2, rows, D), BF),
        vmem((2, 1, GROUP * H), jnp.int32),
        vmem((2, 1, GROUP * H), jnp.int32),
        pltpu.SemaphoreType.DMA((N_SEMS + 56 * n_ctx,)),
        pltpu.SemaphoreType.REGULAR((4,)),
    ]
    done = pl.pallas_call(
        functools.partial(kernel, z),
        out_shape=sums,
        in_specs=[vm] * 10 + [hbm] * 3,
        out_specs=[vm] * len(sums),
        scratch_shapes=scratch,
        compiler_params=pltpu.CompilerParams(
            collective_id=0, has_side_effects=True, vmem_limit_bytes=VMEM_LIMIT
        ),
        name="step",
    )(
        inputs, cotangent, doc_start, freq, attn_gain, mlp_gain, w_q, w_k, w_v, w_o, w_gate, w_up,
        jnp.swapaxes(w_down, 1, 2),
    )
    outs = pl.pallas_call(
        functools.partial(finish, n_ctx),
        out_shape=outs,
        in_specs=[vm] * len(sums),
        out_specs=[vm] * len(outs),
        compiler_params=pltpu.CompilerParams(vmem_limit_bytes=VMEM_LIMIT),
        name="finish",
    )(*done)
    return (*outs[:-1], jnp.swapaxes(outs[-1], 1, 2))


def solution(mesh):
    in_specs = (
        P(None, ("ctx", "wt"), None),
        P(),
        P("section", None),
        P("section", "wt", None),
        P("section", "wt", None),
        P("section", "wt", None),
        P("section", "wt", None),
        P("section", None),
        P("section", None, "wt"),
        P("section", None, "wt"),
        P("section", "wt", None),
        P(None, ("ctx", "wt"), None),
    )
    out_specs = (
        P("section", None, ("ctx", "wt"), None),
        P("section", None, ("ctx", "wt"), None),
        P("section", "wt"),
        P("section", "wt", None),
        P("section", "wt", None),
        P("section", "wt", None),
        P("section", "wt", None),
        P("section", "wt"),
        P("section", None, "wt"),
        P("section", None, "wt"),
        P("section", "wt", None),
    )
    sizes = dict(mesh.shape)
    return jax.shard_map(
        functools.partial(local, sizes), mesh=mesh, in_specs=in_specs, out_specs=out_specs,
        check_vma=False,
    )
```
